32 devices in a mesh: gx: 16 (over z, y, core), gy: 2 (over x).
Axes of the slice: x: 2, y: 2, z: 4, core: 2. Of those that a mesh axis runs over, the one named last changes fastest.
Arguments:
- planes: bfloat16 [3, 64, 128, 128], P(None, 'gx', 'gy'), may hold values from -6 to 6
- kernel: bfloat16 [3, 3, 3, 16, 128], replicated, may hold values from -0.3125 to 0.3125
- bias: float32 [128], replicated, may hold values from -4 to 4
- cotangent: bfloat16 [64, 128, 128], P('gx', 'gy'), may hold values from -6 to 6
Outputs:
- output: bfloat16 [64, 128, 128], P('gx', 'gy')
- input_grad: bfloat16 [3, 64, 128, 128], P(None, 'gx', 'gy')
- kernel_grad: float32 [3, 3, 3, 16, 128], replicated
- bias_grad: float32 [128], replicated
The draws below stay inside these ranges and needn't reach their ends.
All inputs are finite; a program needn't handle non-finite values.
Results may differ from the reference program's by a relative error of at most 0.001.
Values may be sent and summed in bfloat16 or wider, within the bound.
A program may use at most 64 MiB of HBM per device.

```python
import jax
import jax.numpy as jnp
from jax import lax

C = 128
GROUPS = 8
GW = 16
NX = 64
NY = 128


def shard_levels(rng, shape, pieces, least, largest):
    loudness = 1.0
    for position, blocks in pieces:
        heights = jax.random.uniform(jax.random.fold_in(jax.random.fold_in(rng, 6), position), (blocks,), jnp.float32, least / len(pieces), largest / len(pieces))
        loudness = loudness * jnp.repeat(jnp.exp(heights), shape[position] // blocks).reshape((-1,) + (1,) * (len(shape) - 1 - position))
    return loudness


def centred(rng, shape, spread, limit, cuts=(), dtype=jnp.bfloat16):
    result = jax.random.normal(rng, shape, jnp.float32) * spread
    if len(cuts) > 0:
        result = shard_levels(rng, shape, cuts, -0.22, 0.18) * result
    return jnp.clip(result, min=-limit, max=limit).astype(dtype)


def setup_inputs(seed: int = 0) -> dict:
    arg_keys = jax.random.split(jax.random.key(seed), 5)
    return {
        "planes": centred(arg_keys[0], (3, NX, NY, C), 1.0, 6.0, ((1, 16), (2, 2))),
        "kernel": centred(arg_keys[1], (3, 3, 3, GW, C), (27 * GW) ** -0.5, 0.3125),
        "bias": centred(arg_keys[2], (C,), 1.0, 4.0, (), jnp.float32),
        "cotangent": centred(arg_keys[3], (NX, NY, C), 1.0, 6.0, ((0, 16), (1, 2))),
    }


def reference(planes, kernel, bias, cotangent):
    inputs = planes.astype(jnp.float32)
    slope = cotangent.astype(jnp.float32)
    weights = kernel.astype(jnp.float32).reshape(3, 3, 3, GW, GROUPS, GW)
    scale = 1.0 / jnp.sqrt(jnp.float32(NX * NY))
    forward = jnp.zeros((NX, NY, GROUPS, GW), jnp.float32)
    backward = []
    kernel_rows = []
    slope_groups = slope.reshape(NX, NY, GROUPS, GW)
    for depth in range(3):
        plane = inputs[depth]
        grad_plane = jnp.zeros((NX, NY, GROUPS, GW), jnp.float32)
        for tap_x in range(3):
            for tap_y in range(3):
                moved = jnp.roll(plane, (1 - tap_x, 1 - tap_y), axis=(0, 1)).reshape(NX, NY, GROUPS, GW)
                tap_w = weights[depth, tap_x, tap_y]
                forward = forward + jnp.einsum('abgi,igo->abgo', moved, tap_w)
                back_slope = jnp.roll(slope_groups, (tap_x - 1, tap_y - 1), axis=(0, 1))
                grad_plane = grad_plane + jnp.einsum('abgo,igo->abgi', back_slope, tap_w)
                kernel_rows.append(jnp.einsum('abgi,abgo->igo', moved, slope_groups).reshape(GW, C))
        backward.append(grad_plane.reshape(NX, NY, C))
    output = (forward.reshape(NX, NY, C) + bias).astype(jnp.bfloat16)
    input_grad = jnp.stack(backward).astype(jnp.bfloat16)
    kernel_grad = jnp.stack(kernel_rows).reshape(3, 3, 3, GW, C) * scale
    bias_grad = lax.optimization_barrier(jnp.sum(slope, axis=(0, 1))) * scale
    return (output, input_grad, kernel_grad, bias_grad)
```

```python
import functools

import jax
import jax.numpy as jnp
import numpy as np
from jax import lax
from jax.experimental import pallas as pl
from jax.experimental.pallas import tpu as pltpu
from jax.sharding import PartitionSpec as P

GROUPS = 8
MESH = pl.DeviceIdType.MESH
LOW_X = 4
LOW_Y = 2
PARTS = LOW_X * LOW_Y
OWNERS = PARTS // 2
PIECES = GROUPS // OWNERS
F32 = jnp.float32
BF16 = jnp.bfloat16


def kernel_body(
    nx, ny, scale, chunk,
    planes_hbm, kernel_hbm, bias_hbm, cot_hbm,
    out_ref, grad_ref, sums_ref,
    planes, taps, bias, cot, edges, edge_halo, cot_halo, planes_halo,
    weights, weights_back, planes_t, cot_views, planes_views,
    part, recv_a, recv_b,
    local_sem, halo_send, halo_recv, a_send, a_recv, b_send, b_recv, c_send, c_recv,
):
    depth, wx, wy, ch = planes.shape
    cells = wx * wy
    gw = ch // GROUPS
    gx = lax.axis_index("gx")
    gy = lax.axis_index("gy")
    nb = (nx // LOW_X) * (ny // LOW_Y)
    high_y = ny // LOW_Y
    low_gx, low_gy = lax.rem(gx, LOW_X), lax.rem(gy, LOW_Y)
    high_gx, high_gy = lax.div(gx, LOW_X), lax.div(gy, LOW_Y)
    ia = low_gx * LOW_Y + low_gy
    ib = high_gx * high_y + high_gy
    peers_a = [None]
    for k in range(1, PARTS):
        j = lax.rem(ia + k, PARTS)
        peers_a.append((j, (high_gx * LOW_X + lax.div(j, LOW_Y), high_gy * LOW_Y + lax.rem(j, LOW_Y))))
    peers_b = [None]
    for k in range(1, nb):
        j = lax.rem(ib + k, nb)
        peers_b.append((lax.div(j, high_y) * LOW_X + low_gx, lax.rem(j, high_y) * LOW_Y + low_gy))
    around_x = {-1: lax.rem(gx + nx - 1, nx), 0: gx, 1: lax.rem(gx + 1, nx)}
    around_y = {-1: lax.rem(gy + ny - 1, ny), 0: gy, 1: lax.rem(gy + 1, ny)}

    def peer_a(k):
        return peers_a[k]

    def peer_b(k):
        return peers_b[k]

    def near(dx, dy):
        return (around_x[dx], around_y[dy])

    partners = [peer_a(k)[1] for k in range(1, PARTS)] + [peer_b(k) for k in range(1, nb)]
    for dy in ((0, 1) if ny == 2 else (-1, 0, 1)):
        for dx in (-1, 0, 1):
            if (dx, dy) != (0, 0):
                partners.append(near(dx, dy))
    in_cot = pltpu.make_async_copy(cot_hbm, cot, local_sem.at[0])
    in_planes = pltpu.make_async_copy(planes_hbm, planes, local_sem.at[1])
    in_taps = pltpu.make_async_copy(kernel_hbm, taps, local_sem.at[2])
    in_cot.start()
    in_planes.start()
    in_taps.start()
    in_bias = pltpu.make_async_copy(bias_hbm, bias, local_sem.at[3])
    in_bias.start()
    barrier = pltpu.get_barrier_semaphore()
    for where in partners:
        pl.semaphore_signal(barrier, inc=1, device_id=where, device_id_type=MESH)

    in_cot.wait()
    in_planes.wait()

    rows = [(planes, (z, x)) for z in range(depth) for x in range(wx)] + [(cot, (x,)) for x in range(wx)]
    lane_row = lax.broadcasted_iota(jnp.int32, (16, ch), 0)
    low = jnp.zeros((16, ch), F32)
    high = jnp.zeros((16, ch), F32)
    for r, (ref, at) in enumerate(rows):
        first = ref[at + (slice(0, 16),)].astype(F32)[0:1]
        last = ref[at + (slice(wy - 16, wy),)].astype(F32)[15:16]
        low = jnp.where(lane_row == r, first, low)
        high = jnp.where(lane_row == r, last, high)
    edges[0] = low.astype(BF16)
    edges[1] = high.astype(BF16)

    pl.semaphore_wait(barrier, len(partners))

    def remote(src, dst, send, recv, where):
        copy = pltpu.make_async_remote_copy(
            src_ref=src, dst_ref=dst, send_sem=send, recv_sem=recv, device_id=where, device_id_type=MESH
        )
        copy.start()
        return copy

    cot_copies = [
        remote(cot.at[0], cot_halo.at[1], halo_send.at[0], halo_recv.at[0], near(-1, 0)),
        remote(cot.at[wx - 1], cot_halo.at[0], halo_send.at[1], halo_recv.at[1], near(1, 0)),
    ]
    number = 2
    for side, dy in ((1, -1), (0, 1)):
        for dx in (-1, 0, 1):
            cot_copies.append(
                remote(edges.at[1 - side], edge_halo.at[side, 1 - dx], halo_send.at[number], halo_recv.at[number], near(dx, dy))
            )
            number += 1
    planes_copies = [
        remote(planes.at[:, 0], planes_halo.at[1], halo_send.at[8], halo_recv.at[8], near(-1, 0)),
        remote(planes.at[:, wx - 1], planes_halo.at[0], halo_send.at[9], halo_recv.at[9], near(1, 0)),
    ]

    row_group = lax.broadcasted_iota(jnp.int32, (ch, ch), 0) // gw
    col_group = lax.broadcasted_iota(jnp.int32, (ch, ch), 1) // gw
    mask = row_group == col_group
    mask_w = jnp.where(mask, 1.0, 0.0).astype(BF16)
    for z in range(depth):
        planes_t[z * ch : (z + 1) * ch, :] = planes[z].reshape(cells, ch).astype(F32).T.astype(BF16)
    spread = jnp.sum(cot[...].reshape(cells, ch).astype(F32), axis=0, keepdims=True)
    whole_row = lax.broadcasted_iota(jnp.int32, (wy, ch), 0)

    def views(target, row, value, left, right):
        value32 = value.astype(F32)
        here = slice(row * wy, (row + 1) * wy)
        target[here, ch : 2 * ch] = value
        target[here, 0:ch] = jnp.where(whole_row == 0, left, pltpu.roll(value32, 1, 0)).astype(BF16)
        target[here, 2 * ch : 3 * ch] = jnp.where(whole_row == wy - 1, right, pltpu.roll(value32, wy - 1, 0)).astype(BF16)

    def side_of(row):
        if row == 0:
            return 0, wx - 1
        if row == wx + 1:
            return 2, 0
        return 1, row - 1

    for copy in cot_copies:
        copy.wait_recv()
    halo32 = [[edge_halo[s, o].astype(F32) for o in range(3)] for s in range(2)]
    for row in range(wx + 2):
        origin, x = side_of(row)
        value = cot_halo[0] if row == 0 else cot_halo[1] if row == wx + 1 else cot[x]
        r = depth * wx + x
        views(cot_views, row, value, halo32[0][origin][r : r + 1], halo32[1][origin][r : r + 1])

    def put(row, value):
        part[row // chunk, row % chunk : row % chunk + 8, :] = value

    for a in range(3):
        full = jnp.dot(
            planes_t[...], cot_views[(2 - a) * wy : (2 - a) * wy + cells, :], preferred_element_type=F32
        )
        for z in range(depth):
            for b in range(3):
                block = full[z * ch : (z + 1) * ch, (2 - b) * ch : (3 - b) * ch]
                block = jnp.where(mask, block, 0.0).reshape(GROUPS, gw, ch).sum(axis=0)
                start = ((z * 3 + a) * 3 + b) * gw
                put(start, block[0:8])
                put(start + 8, block[8:16])
    base = depth * 9 * gw
    put(base, jnp.broadcast_to(spread, (8, ch)))
    for row in range(base + 8, PARTS * chunk, 8):
        put(row, jnp.zeros((8, ch), F32))

    pieces = [slice(0, 32), slice(32, chunk)]
    a_copies = [[], []]
    for h, rows in enumerate(pieces):
        for k in range(1, PARTS):
            j, where = peer_a(k)
            a_copies[h].append(
                remote(part.at[j, rows], recv_a.at[k - 1, rows], a_send.at[h, k - 1], a_recv.at[h, k - 1], where)
            )

    in_taps.wait()
    in_bias.wait()
    for z in range(depth):
        for a in range(3):
            for b in range(3):
                tile = jnp.concatenate([taps[z, a, b]] * GROUPS, axis=0) * mask_w
                weights[z, a, b * ch : (b + 1) * ch, :] = tile
                weights_back[a, z * ch : (z + 1) * ch, (2 - b) * ch : (3 - b) * ch] = tile
    for copy in planes_copies:
        copy.wait_recv()
    for z in range(depth):
        for row in range(wx + 2):
            origin, x = side_of(row)
            value = planes_halo[0, z] if row == 0 else planes_halo[1, z] if row == wx + 1 else planes[z, x]
            r = z * wx + x
            views(planes_views.at[z], row, value, halo32[0][origin][r : r + 1], halo32[1][origin][r : r + 1])
    forward = jnp.zeros((cells, ch), F32)
    for z in range(depth):
        for a in range(3):
            forward = forward + jnp.dot(
                planes_views[z, a * wy : a * wy + cells, :], weights[z, a], preferred_element_type=F32
            )
    out_ref[...] = (forward + bias[...]).astype(BF16).reshape(wx, wy, ch)

    b_copies = [[], []]
    for h, rows in enumerate(pieces):
        for copy in a_copies[h]:
            copy.wait_recv()
        reduced = part[ia, rows]
        for k in range(PARTS - 1):
            reduced = reduced + recv_a[k, rows]
        recv_b[ib, rows] = reduced
        for k in range(1, nb):
            b_copies[h].append(
                remote(recv_b.at[ib, rows], recv_b.at[ib, rows], b_send.at[h, k - 1], b_recv.at[h, k - 1], peer_b(k))
            )

    slopes = jnp.zeros((cells, depth * ch), F32)
    for a in range(3):
        slopes = slopes + lax.dot_general(
            cot_views[(2 - a) * wy : (2 - a) * wy + cells, :],
            weights_back[a],
            (((1,), (1,)), ((), ())),
            preferred_element_type=F32,
        )
    for z in range(depth):
        grad_ref[z] = slopes[:, z * ch : (z + 1) * ch].astype(BF16).reshape(wx, wy, ch)

    c_copies = []
    for h, rows in enumerate(pieces):
        for copy in b_copies[h]:
            copy.wait_recv()
        value = recv_b[0, rows]
        for k in range(1, nb):
            value = value + recv_b[k, rows]
        sums_ref[ia, rows] = value * scale
        for k in range(1, PARTS):
            _, where = peer_a(k)
            c_copies.append(
                remote(sums_ref.at[ia, rows], sums_ref.at[ia, rows], c_send.at[h, k - 1], c_recv.at[h, k - 1], where)
            )

    for copy in cot_copies + planes_copies + sum(a_copies + b_copies, []):
        copy.wait_send()
    for copy in c_copies:
        copy.wait()

def owner_body(
    nx, scale,
    planes_hbm, kernel_hbm, bias_hbm, cot_hbm,
    out_ref, grad_ref, sums_ref,
    planes, taps, bias, cot, edges, edge_halo, cot_halo, planes_halo,
    weights, weights_back, cot_views, planes_views,
    slabs, recv_a, row_halo, left, right, recv_b, recv_c,
    local_sem, halo_send, halo_recv, a_send, a_recv, z_send, z_recv, b_send, b_recv, c_send, c_recv,
):
    depth, wx, wy, ch = planes.shape
    cells = wx * wy
    gw = ch // GROUPS
    lanes = 2 * wy
    rows_x = LOW_X * wx
    nb = nx // LOW_X
    gx = lax.axis_index("gx")
    gy = lax.axis_index("gy")
    blk, r = lax.div(gx, LOW_X), lax.rem(gx, LOW_X)
    me = r * 2 + gy
    owns = lax.rem(r, 2) == 1
    mine = lax.div(r, 2) * 2 + gy
    above, below = lax.rem(blk + 1, nb), lax.rem(blk + nb - 1, nb)

    def device(block, index):
        return (block * LOW_X + lax.div(index, 2), lax.rem(index, 2))

    def owner(block, q):
        return (block * LOW_X + 2 * lax.div(q, 2) + 1, lax.rem(q, 2))

    around_x = {-1: lax.rem(gx + nx - 1, nx), 0: gx, 1: lax.rem(gx + 1, nx)}

    def near(dx, dy):
        return (around_x[dx], lax.rem(gy + dy + 2, 2))

    in_cot = pltpu.make_async_copy(cot_hbm, cot, local_sem.at[0])
    in_planes = [pltpu.make_async_copy(planes_hbm.at[z], planes.at[z], local_sem.at[1 + z]) for z in range(depth)]
    in_taps = pltpu.make_async_copy(kernel_hbm, taps, local_sem.at[1 + depth])
    in_bias = pltpu.make_async_copy(bias_hbm, bias, local_sem.at[2 + depth])
    in_cot.start()
    for copy in in_planes:
        copy.start()
    in_taps.start()
    in_bias.start()
    barrier = pltpu.get_barrier_semaphore()

    def greet(where):
        pl.semaphore_signal(barrier, inc=1, device_id=where, device_id_type=MESH)

    @pl.when(owns)
    def _():
        for k in range(1, PARTS):
            greet(device(blk, lax.rem(me + k, PARTS)))
        for c in range(2):
            greet(device(above, c))
            greet(device(below, PARTS - 2 + c))
        for k in range(1, nb):
            greet(device(lax.rem(blk + k, nb), me))

    @pl.when(jnp.logical_not(owns))
    def _():
        for q in range(OWNERS):
            greet(owner(blk, q))

    neighbours = [near(dx, dy) for dy in (0, 1) for dx in (-1, 0, 1) if (dx, dy) != (0, 0)]
    for where in neighbours:
        greet(where)

    in_cot.wait()
    slabs[:, depth * gw :, :] = cot[...].reshape(cells, ch).astype(F32).T.astype(BF16).reshape(GROUPS, gw, cells)
    for z in range(depth):
        in_planes[z].wait()
        slabs[:, z * gw : (z + 1) * gw, :] = planes[z].reshape(cells, ch).astype(F32).T.astype(BF16).reshape(GROUPS, gw, cells)

    at_end = jnp.logical_or(r == 0, r == LOW_X - 1)
    pl.semaphore_wait(
        barrier, len(neighbours) + jnp.where(owns, PARTS - 1 + nb - 1, OWNERS) + jnp.where(at_end, OWNERS, 0)
    )

    def remote(src, dst, send, recv, where):
        return pltpu.make_async_remote_copy(
            src_ref=src, dst_ref=dst, send_sem=send, recv_sem=recv, device_id=where, device_id_type=MESH
        )

    def row_copy(side, h, q):
        part = (slice(depth * gw, (depth + 1) * gw), slice((1 - side) * (cells - lanes), (1 - side) * (cells - lanes) + lanes))
        return remote(
            slabs.at[(h * OWNERS + q,) + part], row_halo.at[h, side, gy],
            z_send.at[h, q], z_recv.at[h, side, gy], owner((above, below)[side], q),
        )

    def slab_copy(h, q):
        return remote(slabs.at[h * OWNERS + q], recv_a.at[h, me], a_send.at[h, q], a_recv.at[h, me], owner(blk, q))

    def own_slab(h):
        return pltpu.make_async_copy(slabs.at[h * OWNERS + mine], recv_a.at[h, me], a_recv.at[h, me])

    for h in range(PIECES):
        for side, edge in ((0, LOW_X - 1), (1, 0)):
            @pl.when(r == edge)
            def _(h=h, side=side):
                for q in range(OWNERS):
                    row_copy(side, h, q).start()

        @pl.when(owns)
        def _(h=h):
            for k in range(1, OWNERS):
                slab_copy(h, lax.rem(mine + k, OWNERS)).start()
            own_slab(h).start()

        @pl.when(jnp.logical_not(owns))
        def _(h=h):
            for q in range(OWNERS):
                slab_copy(h, q).start()

    rows = [(planes, (z, x)) for z in range(depth) for x in range(wx)] + [(cot, (x,)) for x in range(wx)]
    lane_row = lax.broadcasted_iota(jnp.int32, (16, ch), 0)
    low = jnp.zeros((16, ch), F32)
    high = jnp.zeros((16, ch), F32)
    for n, (ref, at) in enumerate(rows):
        first = ref[at + (slice(0, 16),)].astype(F32)[0:1]
        last = ref[at + (slice(wy - 16, wy),)].astype(F32)[15:16]
        low = jnp.where(lane_row == n, first, low)
        high = jnp.where(lane_row == n, last, high)
    edges[0] = low.astype(BF16)
    edges[1] = high.astype(BF16)

    halo_copies = [
        remote(cot.at[0], cot_halo.at[1], halo_send.at[0], halo_recv.at[0], near(-1, 0)),
        remote(cot.at[wx - 1], cot_halo.at[0], halo_send.at[1], halo_recv.at[1], near(1, 0)),
        remote(planes.at[:, 0], planes_halo.at[1], halo_send.at[8], halo_recv.at[8], near(-1, 0)),
        remote(planes.at[:, wx - 1], planes_halo.at[0], halo_send.at[9], halo_recv.at[9], near(1, 0)),
    ]
    number = 2
    for side, dy in ((1, -1), (0, 1)):
        for dx in (-1, 0, 1):
            halo_copies.append(
                remote(edges.at[1 - side], edge_halo.at[side, 1 - dx], halo_send.at[number], halo_recv.at[number], near(dx, dy))
            )
            number += 1
    for copy in halo_copies:
        copy.start()

    row_group = lax.broadcasted_iota(jnp.int32, (ch, ch), 0) // gw
    col_group = lax.broadcasted_iota(jnp.int32, (ch, ch), 1) // gw
    mask_w = jnp.where(row_group == col_group, 1.0, 0.0).astype(BF16)
    in_taps.wait()
    in_bias.wait()
    for z in range(depth):
        for a in range(3):
            for b in range(3):
                tile = jnp.concatenate([taps[z, a, b]] * GROUPS, axis=0) * mask_w
                weights[z, a, b * ch : (b + 1) * ch, :] = tile
                weights_back[a, z * ch : (z + 1) * ch, (2 - b) * ch : (3 - b) * ch] = tile

    wide = GROUPS * gw
    lane = lax.broadcasted_iota(jnp.int32, (gw, lanes), 1)
    first_half = lane < wy

    @pl.when(owns)
    def _():
        left[depth * gw :, :] = jnp.ones((gw, left.shape[1]), BF16)

    def merged(g0, g1):
        g0, g1 = g0.astype(F32), g1.astype(F32)
        return (
            jnp.where(first_half, g0, pltpu.roll(g1, wy, 1)),
            jnp.where(first_half, pltpu.roll(g0, wy, 1), g1),
        )

    def gradient_part(h):
        for src in range(PARTS):
            remote(slabs.at[0], recv_a.at[h, src], a_send.at[h, 0], a_recv.at[h, src], device(blk, src)).wait_recv()
        for side in range(2):
            for c in range(2):
                remote(
                    slabs.at[0, 0:gw, 0:lanes], row_halo.at[h, side, c], z_send.at[h, 0], z_recv.at[h, side, c], device(blk, c)
                ).wait_recv()

        def tile(dev, piece, j):
            return recv_a[h, dev, piece * gw : (piece + 1) * gw, j * lanes : (j + 1) * lanes]

        for dev in range(0, PARTS, 2):
            for j in range(wx // 2):
                for z in range(depth):
                    for half, value in enumerate(merged(tile(dev, z, j), tile(dev + 1, z, j))):
                        at = (dev // 2) * wx + 2 * j + half
                        left[z * gw : (z + 1) * gw, at * lanes : (at + 1) * lanes] = value.astype(BF16)

        def spread_row(x, value):
            for b in range(3):
                shifted = value if b == 1 else pltpu.roll(value, 1 if b == 2 else lanes - 1, 1)
                shifted = shifted.astype(BF16)
                for a in range(3):
                    u = x + a - 1
                    if 0 <= u < rows_x:
                        where = slice(u * lanes, (u + 1) * lanes)
                        tap = a * 3 + b
                        if tap < 8:
                            right[tap * gw : (tap + 1) * gw, where] = shifted
                        else:
                            for n in range(depth):
                                right[wide + n * gw : wide + (n + 1) * gw, where] = shifted

        spread_row(-1, merged(row_halo[h, 0, 0], row_halo[h, 0, 1])[1])
        spread_row(rows_x, merged(row_halo[h, 1, 0], row_halo[h, 1, 1])[0])
        for dev in range(0, PARTS, 2):
            for j in range(wx // 2):
                for half, value in enumerate(merged(tile(dev, depth, j), tile(dev + 1, depth, j))):
                    spread_row((dev // 2) * wx + 2 * j + half, value)
        full = lax.dot_general(left[...], right[...], (((1,), (1,)), ((), ())), preferred_element_type=F32)
        main, last = full[:, 0:wide], full[:, wide : 2 * wide]
        tail = main[depth * gw :]
        for z in range(depth):
            tail = jnp.where(jnp.logical_and(lane >= z * gw, lane < (z + 1) * gw), last[z * gw : (z + 1) * gw], tail)
        recv_b[h, blk, 0 : depth * gw, :] = main[0 : depth * gw]
        recv_b[h, blk, depth * gw :, :] = tail

    def b_copy(h, k):
        return remote(
            recv_b.at[h, blk], recv_b.at[h, blk], b_send.at[h, k - 1], b_recv.at[h, k - 1], device(lax.rem(blk + k, nb), me)
        )

    @pl.when(owns)
    def _():
        right[wide + depth * gw :, :] = jnp.zeros((right.shape[0] - wide - depth * gw, right.shape[1]), BF16)
        for h in range(PIECES):
            gradient_part(h)
            for k in range(1, nb):
                b_copy(h, k).start()

    whole_row = lax.broadcasted_iota(jnp.int32, (wy, ch), 0)

    def views(target, row, value, before, after):
        value32 = value.astype(F32)
        here = slice(row * wy, (row + 1) * wy)
        target[here, ch : 2 * ch] = value
        target[here, 0:ch] = jnp.where(whole_row == 0, before, pltpu.roll(value32, 1, 0)).astype(BF16)
        target[here, 2 * ch : 3 * ch] = jnp.where(whole_row == wy - 1, after, pltpu.roll(value32, wy - 1, 0)).astype(BF16)

    def side_of(row):
        if row == 0:
            return 0, wx - 1
        if row == wx + 1:
            return 2, 0
        return 1, row - 1

    for copy in halo_copies:
        copy.wait_recv()
    halo32 = [[edge_halo[s, o].astype(F32) for o in range(3)] for s in range(2)]
    for row in range(wx + 2):
        origin, x = side_of(row)
        value = cot_halo[0] if row == 0 else cot_halo[1] if row == wx + 1 else cot[x]
        n = depth * wx + x
        views(cot_views, row, value, halo32[0][origin][n : n + 1], halo32[1][origin][n : n + 1])
        for z in range(depth):
            value = planes_halo[0, z] if row == 0 else planes_halo[1, z] if row == wx + 1 else planes[z, x]
            n = z * wx + x
            views(planes_views.at[z], row, value, halo32[0][origin][n : n + 1], halo32[1][origin][n : n + 1])
    forward = jnp.zeros((cells, ch), F32)
    for z in range(depth):
        for a in range(3):
            forward = forward + jnp.dot(
                planes_views[z, a * wy : a * wy + cells, :], weights[z, a], preferred_element_type=F32
            )
    out_ref[...] = (forward + bias[...]).astype(BF16).reshape(wx, wy, ch)
    slopes = jnp.zeros((cells, depth * ch), F32)
    for a in range(3):
        slopes = slopes + lax.dot_general(
            cot_views[(2 - a) * wy : (2 - a) * wy + cells, :],
            weights_back[a],
            (((1,), (1,)), ((), ())),
            preferred_element_type=F32,
        )
    for z in range(depth):
        grad_ref[z] = slopes[:, z * ch : (z + 1) * ch].astype(BF16).reshape(wx, wy, ch)

    def c_copy(h, k):
        g = h * OWNERS + mine
        return remote(
            recv_c.at[g], recv_c.at[g], c_send.at[h, k - 1], c_recv.at[g], device(blk, lax.rem(me + k, PARTS))
        )

    @pl.when(owns)
    def _():
        for h in range(PIECES):
            for k in range(1, nb):
                b_copy(h, k).wait_recv()
            total = recv_b[h, 0]
            for k in range(1, nb):
                total = total + recv_b[h, k]
            g = h * OWNERS + mine
            recv_c[g] = pltpu.roll(total * scale, g * gw, 1)
            for k in range(1, PARTS):
                c_copy(h, k).start()

    for h in range(PIECES):
        for q in range(OWNERS):
            @pl.when(jnp.logical_not(jnp.logical_and(owns, mine == q)))
            def _(h=h, q=q):
                g = h * OWNERS + q
                remote(recv_c.at[g], recv_c.at[g], c_send.at[h, 0], c_recv.at[g], device(blk, 0)).wait_recv()

    slot = lane // gw

    def gathered(rows, shift):
        value = recv_c[(GROUPS - shift) % GROUPS, rows]
        for s in range(1, GROUPS):
            value = jnp.where(slot == s, recv_c[(s - shift) % GROUPS, rows], value)
        return value if shift == 0 else pltpu.roll(value, wide - shift * gw, 1)

    for z in range(depth):
        for tap in range(9):
            at = (z * 9 + tap) * gw
            if tap < 8:
                sums_ref[at : at + gw, :] = gathered(slice(z * gw, (z + 1) * gw), tap)
            else:
                sums_ref[at : at + gw, :] = gathered(slice(depth * gw, (depth + 1) * gw), z)
    at = depth * 9 * gw
    sums_ref[at : at + gw, :] = gathered(slice(depth * gw, (depth + 1) * gw), 4)

    for copy in halo_copies:
        copy.wait_send()
    for side, edge in ((0, LOW_X - 1), (1, 0)):
        @pl.when(r == edge)
        def _(side=side):
            for h in range(PIECES):
                for q in range(OWNERS):
                    row_copy(side, h, q).wait_send()

    @pl.when(owns)
    def _():
        for h in range(PIECES):
            for k in range(1, OWNERS):
                slab_copy(h, lax.rem(mine + k, OWNERS)).wait_send()
            for k in range(1, nb):
                b_copy(h, k).wait_send()
            for k in range(1, PARTS):
                c_copy(h, k).wait_send()

    @pl.when(jnp.logical_not(owns))
    def _():
        for h in range(PIECES):
            for q in range(OWNERS):
                slab_copy(h, q).wait_send()


def place_body(out_from, grad_from, sums, out_to, grad_to, kernel_to, bias_to, sem):
    base = kernel_to.shape[0]
    copies = [
        pltpu.make_async_copy(grad_from, grad_to, sem.at[0]),
        pltpu.make_async_copy(sums.at[0:base], kernel_to, sem.at[1]),
        pltpu.make_async_copy(out_from, out_to, sem.at[2]),
        pltpu.make_async_copy(sums.at[base : base + 1], bias_to, sem.at[3]),
    ]
    for copy in copies:
        copy.start()
    for copy in copies:
        copy.wait()


def by_part(nx, ny, planes, kernel, bias, cotangent):
    depth, wx, wy, ch = planes.shape
    cells = wx * wy
    gw = ch // GROUPS
    nb = (nx // LOW_X) * (ny // LOW_Y)
    needed = depth * 9 * gw + 8
    chunk = -(-needed // (PARTS * 8)) * 8
    scale = np.float32(1.0) / np.sqrt(np.float32(cells * nx * ny))
    dma = pltpu.SemaphoreType.DMA
    vmem = pl.BlockSpec(memory_space=pltpu.VMEM)
    hbm = pl.BlockSpec(memory_space=pltpu.HBM)
    out, grad, sums = pl.pallas_call(
        functools.partial(kernel_body, nx, ny, scale, chunk),
        out_shape=(
            jax.ShapeDtypeStruct((wx, wy, ch), BF16),
            jax.ShapeDtypeStruct((depth, wx, wy, ch), BF16),
            jax.ShapeDtypeStruct((PARTS, chunk, ch), F32),
        ),
        in_specs=[hbm, hbm, hbm, hbm],
        out_specs=(vmem,) * 3,
        scratch_shapes=[
            pltpu.VMEM((depth, wx, wy, ch), BF16),
            pltpu.VMEM((depth, 3, 3, gw, ch), BF16),
            pltpu.VMEM((1, ch), F32),
            pltpu.VMEM((wx, wy, ch), BF16),
            pltpu.VMEM((2, 16, ch), BF16),
            pltpu.VMEM((2, 3, 16, ch), BF16),
            pltpu.VMEM((2, wy, ch), BF16),
            pltpu.VMEM((2, depth, wy, ch), BF16),
            pltpu.VMEM((depth, 3, 3 * ch, ch), BF16),
            pltpu.VMEM((3, depth * ch, 3 * ch), BF16),
            pltpu.VMEM((depth * ch, cells), BF16),
            pltpu.VMEM(((wx + 2) * wy, 3 * ch), BF16),
            pltpu.VMEM((depth, (wx + 2) * wy, 3 * ch), BF16),
            pltpu.VMEM((PARTS, chunk, ch), F32),
            pltpu.VMEM((PARTS - 1, chunk, ch), F32),
            pltpu.VMEM((nb, chunk, ch), F32),
            dma((4,)), dma((10,)), dma((10,)),
            dma((2, PARTS - 1)), dma((2, PARTS - 1)),
            dma((2, max(nb - 1, 1))), dma((2, max(nb - 1, 1))),
            dma((2, PARTS - 1)), dma((2, PARTS - 1)),
        ],
        compiler_params=pltpu.CompilerParams(
            collective_id=0, has_side_effects=True, vmem_limit_bytes=32 * 1024 * 1024
        ),
    )(*(pltpu.with_memory_space_constraint(x, pltpu.HBM) for x in (planes, kernel, bias.reshape(1, ch), cotangent)))
    return out, grad, sums.reshape(PARTS * chunk, ch)


def by_owner(nx, planes, kernel, bias, cotangent):
    depth, wx, wy, ch = planes.shape
    cells = wx * wy
    gw = ch // GROUPS
    lanes = 2 * wy
    nb = nx // LOW_X
    scale = np.float32(1.0) / np.sqrt(np.float32(cells * nx * 2))
    dma = pltpu.SemaphoreType.DMA
    vmem = pl.BlockSpec(memory_space=pltpu.VMEM)
    hbm = pl.BlockSpec(memory_space=pltpu.HBM)
    return pl.pallas_call(
        functools.partial(owner_body, nx, scale),
        out_shape=(
            jax.ShapeDtypeStruct((wx, wy, ch), BF16),
            jax.ShapeDtypeStruct((depth, wx, wy, ch), BF16),
            jax.ShapeDtypeStruct((depth * 9 * gw + gw, ch), F32),
        ),
        in_specs=[hbm, hbm, hbm, hbm],
        out_specs=(vmem,) * 3,
        scratch_shapes=[
            pltpu.VMEM((depth, wx, wy, ch), BF16),
            pltpu.VMEM((depth, 3, 3, gw, ch), BF16),
            pltpu.VMEM((1, ch), F32),
            pltpu.VMEM((wx, wy, ch), BF16),
            pltpu.VMEM((2, 16, ch), BF16),
            pltpu.VMEM((2, 3, 16, ch), BF16),
            pltpu.VMEM((2, wy, ch), BF16),
            pltpu.VMEM((2, depth, wy, ch), BF16),
            pltpu.VMEM((depth, 3, 3 * ch, ch), BF16),
            pltpu.VMEM((3, depth * ch, 3 * ch), BF16),
            pltpu.VMEM(((wx + 2) * wy, 3 * ch), BF16),
            pltpu.VMEM((depth, (wx + 2) * wy, 3 * ch), BF16),
            pltpu.VMEM((GROUPS, (depth + 1) * gw, cells), BF16),
            pltpu.VMEM((PIECES, PARTS, (depth + 1) * gw, cells), BF16),
            pltpu.VMEM((PIECES, 2, 2, gw, lanes), BF16),
            pltpu.VMEM(((depth + 1) * gw, LOW_X * wx * lanes), BF16),
            pltpu.VMEM((2 * ch, LOW_X * wx * lanes), BF16),
            pltpu.VMEM((PIECES, nb, (depth + 1) * gw, ch), F32),
            pltpu.VMEM((GROUPS, (depth + 1) * gw, ch), F32),
            dma((3 + depth,)), dma((10,)), dma((10,)),
            dma((PIECES, OWNERS)), dma((PIECES, PARTS)),
            dma((PIECES, OWNERS)), dma((PIECES, 2, 2)),
            dma((PIECES, nb - 1)), dma((PIECES, nb - 1)),
            dma((PIECES, PARTS - 1)), dma((GROUPS,)),
        ],
        compiler_params=pltpu.CompilerParams(
            collective_id=0, has_side_effects=True, vmem_limit_bytes=32 * 1024 * 1024
        ),
    )(*(pltpu.with_memory_space_constraint(x, pltpu.HBM) for x in (planes, kernel, bias.reshape(1, ch), cotangent)))


def shards(nx, ny, planes, kernel, bias, cotangent):
    depth, wx, wy, ch = planes.shape
    gw = ch // GROUPS
    if ny == 2 and nx % LOW_X == 0 and nx > LOW_X and (depth, wx, 2 * wy, ch, gw) == (3, 4, 128, 128, 16):
        out, grad, sums = by_owner(nx, planes, kernel, bias, cotangent)
    else:
        out, grad, sums = by_part(nx, ny, planes, kernel, bias, cotangent)
    dma = pltpu.SemaphoreType.DMA
    vmem = pl.BlockSpec(memory_space=pltpu.VMEM)
    hbm = pl.BlockSpec(memory_space=pltpu.HBM)
    base = depth * 9 * gw
    out, grad, kernel_grad, bias_grad = pl.pallas_call(
        place_body,
        out_shape=(
            jax.ShapeDtypeStruct(out.shape, BF16),
            jax.ShapeDtypeStruct(grad.shape, BF16),
            jax.ShapeDtypeStruct((base, ch), F32),
            jax.ShapeDtypeStruct((1, ch), F32),
        ),
        in_specs=[vmem] * 3,
        out_specs=(hbm, hbm, hbm, hbm),
        scratch_shapes=[dma((4,))],
    )(*(pltpu.with_memory_space_constraint(x, pltpu.VMEM) for x in (out, grad, sums)))
    return out, grad, kernel_grad.reshape(kernel.shape), bias_grad.reshape(ch)


def solution(mesh):
    in_specs = (P(None, "gx", "gy", None), P(), P(), P("gx", "gy", None))
    out_specs = (P("gx", "gy", None), P(None, "gx", "gy", None), P(), P())
    body = functools.partial(shards, mesh.shape["gx"], mesh.shape["gy"])
    return jax.shard_map(body, mesh=mesh, in_specs=in_specs, out_specs=out_specs, check_vma=False)
```

```python
import functools

import jax
import jax.numpy as jnp
import numpy as np
from jax import lax
from jax.experimental import pallas as pl
from jax.experimental.pallas import tpu as pltpu
from jax.sharding import PartitionSpec as P

GROUPS = 8
MESH = pl.DeviceIdType.MESH
LOW_X = 4
LOW_Y = 2
PARTS = LOW_X * LOW_Y
OWNERS = PARTS // 2
PIECES = GROUPS // OWNERS
F32 = jnp.float32
BF16 = jnp.bfloat16


def kernel_body(
    nx, ny, scale, chunk,
    planes_hbm, kernel_hbm, bias_hbm, cot_hbm,
    out_ref, grad_ref, sums_ref,
    planes, taps, bias, cot, edges, edge_halo, cot_halo, planes_halo,
    weights, weights_back, planes_t, cot_views, planes_views,
    part, recv_a, recv_b,
    local_sem, halo_send, halo_recv, a_send, a_recv, b_send, b_recv, c_send, c_recv,
):
    depth, wx, wy, ch = planes.shape
    cells = wx * wy
    gw = ch // GROUPS
    gx = lax.axis_index("gx")
    gy = lax.axis_index("gy")
    nb = (nx // LOW_X) * (ny // LOW_Y)
    high_y = ny // LOW_Y
    low_gx, low_gy = lax.rem(gx, LOW_X), lax.rem(gy, LOW_Y)
    high_gx, high_gy = lax.div(gx, LOW_X), lax.div(gy, LOW_Y)
    ia = low_gx * LOW_Y + low_gy
    ib = high_gx * high_y + high_gy
    peers_a = [None]
    for k in range(1, PARTS):
        j = lax.rem(ia + k, PARTS)
        peers_a.append((j, (high_gx * LOW_X + lax.div(j, LOW_Y), high_gy * LOW_Y + lax.rem(j, LOW_Y))))
    peers_b = [None]
    for k in range(1, nb):
        j = lax.rem(ib + k, nb)
        peers_b.append((lax.div(j, high_y) * LOW_X + low_gx, lax.rem(j, high_y) * LOW_Y + low_gy))
    around_x = {-1: lax.rem(gx + nx - 1, nx), 0: gx, 1: lax.rem(gx + 1, nx)}
    around_y = {-1: lax.rem(gy + ny - 1, ny), 0: gy, 1: lax.rem(gy + 1, ny)}

    def peer_a(k):
        return peers_a[k]

    def peer_b(k):
        return peers_b[k]

    def near(dx, dy):
        return (around_x[dx], around_y[dy])

    partners = [peer_a(k)[1] for k in range(1, PARTS)] + [peer_b(k) for k in range(1, nb)]
    for dy in ((0, 1) if ny == 2 else (-1, 0, 1)):
        for dx in (-1, 0, 1):
            if (dx, dy) != (0, 0):
                partners.append(near(dx, dy))
    in_cot = pltpu.make_async_copy(cot_hbm, cot, local_sem.at[0])
    in_planes = pltpu.make_async_copy(planes_hbm, planes, local_sem.at[1])
    in_taps = pltpu.make_async_copy(kernel_hbm, taps, local_sem.at[2])
    in_cot.start()
    in_planes.start()
    in_taps.start()
    in_bias = pltpu.make_async_copy(bias_hbm, bias, local_sem.at[3])
    in_bias.start()
    barrier = pltpu.get_barrier_semaphore()
    for where in partners:
        pl.semaphore_signal(barrier, inc=1, device_id=where, device_id_type=MESH)

    in_cot.wait()
    in_planes.wait()

    rows = [(planes, (z, x)) for z in range(depth) for x in range(wx)] + [(cot, (x,)) for x in range(wx)]
    lane_row = lax.broadcasted_iota(jnp.int32, (16, ch), 0)
    low = jnp.zeros((16, ch), F32)
    high = jnp.zeros((16, ch), F32)
    for r, (ref, at) in enumerate(rows):
        first = ref[at + (slice(0, 16),)].astype(F32)[0:1]
        last = ref[at + (slice(wy - 16, wy),)].astype(F32)[15:16]
        low = jnp.where(lane_row == r, first, low)
        high = jnp.where(lane_row == r, last, high)
    edges[0] = low.astype(BF16)
    edges[1] = high.astype(BF16)

    pl.semaphore_wait(barrier, len(partners))

    def remote(src, dst, send, recv, where):
        copy = pltpu.make_async_remote_copy(
            src_ref=src, dst_ref=dst, send_sem=send, recv_sem=recv, device_id=where, device_id_type=MESH
        )
        copy.start()
        return copy

    cot_copies = [
        remote(cot.at[0], cot_halo.at[1], halo_send.at[0], halo_recv.at[0], near(-1, 0)),
        remote(cot.at[wx - 1], cot_halo.at[0], halo_send.at[1], halo_recv.at[1], near(1, 0)),
    ]
    number = 2
    for side, dy in ((1, -1), (0, 1)):
        for dx in (-1, 0, 1):
            cot_copies.append(
                remote(edges.at[1 - side], edge_halo.at[side, 1 - dx], halo_send.at[number], halo_recv.at[number], near(dx, dy))
            )
            number += 1
    planes_copies = [
        remote(planes.at[:, 0], planes_halo.at[1], halo_send.at[8], halo_recv.at[8], near(-1, 0)),
        remote(planes.at[:, wx - 1], planes_halo.at[0], halo_send.at[9], halo_recv.at[9], near(1, 0)),
    ]

    row_group = lax.broadcasted_iota(jnp.int32, (ch, ch), 0) // gw
    col_group = lax.broadcasted_iota(jnp.int32, (ch, ch), 1) // gw
    mask = row_group == col_group
    mask_w = jnp.where(mask, 1.0, 0.0).astype(BF16)
    for z in range(depth):
        planes_t[z * ch : (z + 1) * ch, :] = planes[z].reshape(cells, ch).astype(F32).T.astype(BF16)
    spread = jnp.sum(cot[...].reshape(cells, ch).astype(F32), axis=0, keepdims=True)
    whole_row = lax.broadcasted_iota(jnp.int32, (wy, ch), 0)

    def views(target, row, value, left, right):
        value32 = value.astype(F32)
        here = slice(row * wy, (row + 1) * wy)
        target[here, ch : 2 * ch] = value
        target[here, 0:ch] = jnp.where(whole_row == 0, left, pltpu.roll(value32, 1, 0)).astype(BF16)
        target[here, 2 * ch : 3 * ch] = jnp.where(whole_row == wy - 1, right, pltpu.roll(value32, wy - 1, 0)).astype(BF16)

    def side_of(row):
        if row == 0:
            return 0, wx - 1
        if row == wx + 1:
            return 2, 0
        return 1, row - 1

    for copy in cot_copies:
        copy.wait_recv()
    halo32 = [[edge_halo[s, o].astype(F32) for o in range(3)] for s in range(2)]
    for row in range(wx + 2):
        origin, x = side_of(row)
        value = cot_halo[0] if row == 0 else cot_halo[1] if row == wx + 1 else cot[x]
        r = depth * wx + x
        views(cot_views, row, value, halo32[0][origin][r : r + 1], halo32[1][origin][r : r + 1])

    def put(row, value):
        part[row // chunk, row % chunk : row % chunk + 8, :] = value

    for a in range(3):
        full = jnp.dot(
            planes_t[...], cot_views[(2 - a) * wy : (2 - a) * wy + cells, :], preferred_element_type=F32
        )
        for z in range(depth):
            for b in range(3):
                block = full[z * ch : (z + 1) * ch, (2 - b) * ch : (3 - b) * ch]
                block = jnp.where(mask, block, 0.0).reshape(GROUPS, gw, ch).sum(axis=0)
                start = ((z * 3 + a) * 3 + b) * gw
                put(start, block[0:8])
                put(start + 8, block[8:16])
    base = depth * 9 * gw
    put(base, jnp.broadcast_to(spread, (8, ch)))
    for row in range(base + 8, PARTS * chunk, 8):
        put(row, jnp.zeros((8, ch), F32))

    pieces = [slice(0, 32), slice(32, chunk)]
    a_copies = [[], []]
    for h, rows in enumerate(pieces):
        for k in range(1, PARTS):
            j, where = peer_a(k)
            a_copies[h].append(
                remote(part.at[j, rows], recv_a.at[k - 1, rows], a_send.at[h, k - 1], a_recv.at[h, k - 1], where)
            )

    in_taps.wait()
    in_bias.wait()
    for z in range(depth):
        for a in range(3):
            for b in range(3):
                tile = jnp.concatenate([taps[z, a, b]] * GROUPS, axis=0) * mask_w
                weights[z, a, b * ch : (b + 1) * ch, :] = tile
                weights_back[a, z * ch : (z + 1) * ch, (2 - b) * ch : (3 - b) * ch] = tile
    for copy in planes_copies:
        copy.wait_recv()
    for z in range(depth):
        for row in range(wx + 2):
            origin, x = side_of(row)
            value = planes_halo[0, z] if row == 0 else planes_halo[1, z] if row == wx + 1 else planes[z, x]
            r = z * wx + x
            views(planes_views.at[z], row, value, halo32[0][origin][r : r + 1], halo32[1][origin][r : r + 1])
    forward = jnp.zeros((cells, ch), F32)
    for z in range(depth):
        for a in range(3):
            forward = forward + jnp.dot(
                planes_views[z, a * wy : a * wy + cells, :], weights[z, a], preferred_element_type=F32
            )
    out_ref[...] = (forward + bias[...]).astype(BF16).reshape(wx, wy, ch)

    b_copies = [[], []]
    for h, rows in enumerate(pieces):
        for copy in a_copies[h]:
            copy.wait_recv()
        reduced = part[ia, rows]
        for k in range(PARTS - 1):
            reduced = reduced + recv_a[k, rows]
        recv_b[ib, rows] = reduced
        for k in range(1, nb):
            b_copies[h].append(
                remote(recv_b.at[ib, rows], recv_b.at[ib, rows], b_send.at[h, k - 1], b_recv.at[h, k - 1], peer_b(k))
            )

    slopes = jnp.zeros((cells, depth * ch), F32)
    for a in range(3):
        slopes = slopes + lax.dot_general(
            cot_views[(2 - a) * wy : (2 - a) * wy + cells, :],
            weights_back[a],
            (((1,), (1,)), ((), ())),
            preferred_element_type=F32,
        )
    for z in range(depth):
        grad_ref[z] = slopes[:, z * ch : (z + 1) * ch].astype(BF16).reshape(wx, wy, ch)

    c_copies = []
    for h, rows in enumerate(pieces):
        for copy in b_copies[h]:
            copy.wait_recv()
        value = recv_b[0, rows]
        for k in range(1, nb):
            value = value + recv_b[k, rows]
        sums_ref[ia, rows] = value * scale
        for k in range(1, PARTS):
            _, where = peer_a(k)
            c_copies.append(
                remote(sums_ref.at[ia, rows], sums_ref.at[ia, rows], c_send.at[h, k - 1], c_recv.at[h, k - 1], where)
            )

    for copy in cot_copies + planes_copies + sum(a_copies + b_copies, []):
        copy.wait_send()
    for copy in c_copies:
        copy.wait()

def owner_body(
    nx, scale,
    planes_hbm, kernel_hbm, bias_hbm, cot_hbm,
    out_ref, grad_ref, sums_ref,
    planes, taps, bias, cot, edges, edge_halo, cot_halo, planes_halo,
    weights, weights_back, cot_views, planes_views,
    slabs, recv_a, row_halo, left, right, recv_b, recv_c,
    local_sem, halo_send, halo_recv, a_send, a_recv, z_send, z_recv, b_send, b_recv, c_send, c_recv, go,
):
    depth, wx, wy, ch = planes.shape
    cells = wx * wy
    gw = ch // GROUPS
    lanes = 2 * wy
    rows_x = LOW_X * wx
    nb = nx // LOW_X
    gx = lax.axis_index("gx")
    gy = lax.axis_index("gy")
    blk, r = lax.div(gx, LOW_X), lax.rem(gx, LOW_X)
    me = r * 2 + gy
    owns = lax.rem(r, 2) == 1
    mine = lax.div(r, 2) * 2 + gy
    above, below = lax.rem(blk + 1, nb), lax.rem(blk + nb - 1, nb)

    def device(block, index):
        return (block * LOW_X + lax.div(index, 2), lax.rem(index, 2))

    def owner(block, q):
        return (block * LOW_X + 2 * lax.div(q, 2) + 1, lax.rem(q, 2))

    around_x = {-1: lax.rem(gx + nx - 1, nx), 0: gx, 1: lax.rem(gx + 1, nx)}

    def near(dx, dy):
        return (around_x[dx], lax.rem(gy + dy + 2, 2))

    in_cot = pltpu.make_async_copy(cot_hbm, cot, local_sem.at[0])
    in_planes = [pltpu.make_async_copy(planes_hbm.at[z], planes.at[z], local_sem.at[1 + z]) for z in range(depth)]
    in_taps = pltpu.make_async_copy(kernel_hbm, taps, local_sem.at[1 + depth])
    in_bias = pltpu.make_async_copy(bias_hbm, bias, local_sem.at[2 + depth])
    in_cot.start()
    for copy in in_planes:
        copy.start()
    in_taps.start()
    in_bias.start()
    barrier = pltpu.get_barrier_semaphore()

    def greet(where):
        pl.semaphore_signal(barrier, inc=1, device_id=where, device_id_type=MESH)

    @pl.when(owns)
    def _():
        for k in range(1, PARTS):
            greet(device(blk, lax.rem(me + k, PARTS)))
        for c in range(2):
            greet(device(below, PARTS - 2 + c))

        @pl.when(blk != nb - 1)
        def _():
            for c in range(2):
                greet(device(above, c))

        @pl.when(blk != 1)
        def _():
            for c in range(2):
                greet(device(below, c))

        @pl.when(blk == 1)
        def _():
            for c in range(2):
                greet(device(nb - 1, PARTS - 2 + c))

    @pl.when(jnp.logical_and(r == 0, blk == 0))
    def _():
        for c in range(2):
            greet(device(nb - 1, PARTS - 2 + c))

    in_cot.wait()
    slabs[:, depth * gw :, :] = cot[...].reshape(cells, ch).astype(F32).T.astype(BF16).reshape(GROUPS, gw, cells)
    for z in range(depth):
        in_planes[z].wait()
        slabs[:, z * gw : (z + 1) * gw, :] = planes[z].reshape(cells, ch).astype(F32).T.astype(BF16).reshape(GROUPS, gw, cells)

    pl.semaphore_wait(
        barrier,
        jnp.where(owns, OWNERS - 1, OWNERS)
        + jnp.where(jnp.logical_and(r == 0, blk != 0), 2 * OWNERS, 0)
        + jnp.where(r == LOW_X - 1, jnp.where(blk == nb - 1, 2 * OWNERS + 2, OWNERS), 0),

    )

    def remote(src, dst, send, recv, where):
        return pltpu.make_async_remote_copy(
            src_ref=src, dst_ref=dst, send_sem=send, recv_sem=recv, device_id=where, device_id_type=MESH
        )

    def row_copy(side, h, q, with_planes=False):
        rows = slice(0 if with_planes else depth * gw, (depth + 1) * gw)
        cols = slice((1 - side) * (cells - lanes), (1 - side) * (cells - lanes) + lanes)
        return remote(
            slabs.at[h * OWNERS + q, rows, cols], row_halo.at[h, side, gy, rows],
            z_send.at[h, q], z_recv.at[h, side, gy], owner((above, below)[side], q),
        )

    def rows_from(side, h, c, with_planes=False):
        rows = slice(0 if with_planes else depth * gw, (depth + 1) * gw)
        return remote(
            slabs.at[0, rows, 0:lanes], row_halo.at[h, side, c, rows], z_send.at[h, 0], z_recv.at[h, side, c], device(blk, c)
        )

    up = jnp.logical_and(r == LOW_X - 1, blk != nb - 1)
    seam = jnp.logical_and(r == LOW_X - 1, blk == nb - 1)
    down = jnp.logical_and(r == 0, blk != 0)
    row_roles = ((up, 0, False), (seam, 0, True), (down, 1, False))

    def slab_copy(h, q):
        return remote(slabs.at[h * OWNERS + q], recv_a.at[h, me], a_send.at[h, q], a_recv.at[h, me], owner(blk, q))

    def own_slab(h):
        return pltpu.make_async_copy(slabs.at[h * OWNERS + mine], recv_a.at[h, me], a_recv.at[h, me])

    for h in range(PIECES):
        for when, side, with_planes in row_roles:
            @pl.when(when)
            def _(h=h, side=side, with_planes=with_planes):
                for q in range(OWNERS):
                    row_copy(side, h, q, with_planes).start()

        @pl.when(owns)
        def _(h=h):
            for k in range(1, OWNERS):
                slab_copy(h, lax.rem(mine + k, OWNERS)).start()
            own_slab(h).start()

        @pl.when(jnp.logical_not(owns))
        def _(h=h):
            for q in range(OWNERS):
                slab_copy(h, q).start()

    rows = [(planes, (z, x)) for z in range(depth) for x in range(wx)] + [(cot, (x,)) for x in range(wx)]
    lane_row = lax.broadcasted_iota(jnp.int32, (16, ch), 0)
    low = jnp.zeros((16, ch), F32)
    high = jnp.zeros((16, ch), F32)
    for n, (ref, at) in enumerate(rows):
        first = ref[at + (slice(0, 16),)].astype(F32)[0:1]
        last = ref[at + (slice(wy - 16, wy),)].astype(F32)[15:16]
        low = jnp.where(lane_row == n, first, low)
        high = jnp.where(lane_row == n, last, high)
    edges[0] = low.astype(BF16)
    edges[1] = high.astype(BF16)

    halo_copies = [
        remote(cot.at[0], cot_halo.at[1], halo_send.at[0], halo_recv.at[0], near(-1, 0)),
        remote(cot.at[wx - 1], cot_halo.at[0], halo_send.at[1], halo_recv.at[1], near(1, 0)),
        remote(planes.at[:, 0], planes_halo.at[1], halo_send.at[8], halo_recv.at[8], near(-1, 0)),
        remote(planes.at[:, wx - 1], planes_halo.at[0], halo_send.at[9], halo_recv.at[9], near(1, 0)),
    ]
    number = 2
    for side, dy in ((1, -1), (0, 1)):
        for dx in (-1, 0, 1):
            halo_copies.append(
                remote(edges.at[1 - side], edge_halo.at[side, 1 - dx], halo_send.at[number], halo_recv.at[number], near(dx, dy))
            )
            number += 1
    row_group = lax.broadcasted_iota(jnp.int32, (ch, ch), 0) // gw
    col_group = lax.broadcasted_iota(jnp.int32, (ch, ch), 1) // gw
    mask_w = jnp.where(row_group == col_group, 1.0, 0.0).astype(BF16)
    in_taps.wait()
    in_bias.wait()
    for z in range(depth):
        for a in range(3):
            for b in range(3):
                tile = jnp.concatenate([taps[z, a, b]] * GROUPS, axis=0) * mask_w
                weights[z, a, b * ch : (b + 1) * ch, :] = tile
                weights_back[a, z * ch : (z + 1) * ch, (2 - b) * ch : (3 - b) * ch] = tile

    wide = GROUPS * gw
    lane = lax.broadcasted_iota(jnp.int32, (gw, lanes), 1)
    first_half = lane < wy

    @pl.when(owns)
    def _():
        left[depth * gw :, :] = jnp.ones((gw, left.shape[1]), BF16)
        right[wide + depth * gw :, :] = jnp.zeros((right.shape[0] - wide - depth * gw, right.shape[1]), BF16)
        right[3 * gw :, 0:lanes] = jnp.zeros((right.shape[0] - 3 * gw, lanes), BF16)

    def merged(g0, g1):
        g0, g1 = g0.astype(F32), g1.astype(F32)
        return (
            jnp.where(first_half, g0, pltpu.roll(g1, wy, 1)),
            jnp.where(first_half, pltpu.roll(g0, wy, 1), g1),
        )

    def gradient_part(h):
        for src in range(PARTS):
            remote(slabs.at[0], recv_a.at[h, src], a_send.at[h, 0], a_recv.at[h, src], device(blk, src)).wait_recv()
        for when, side, with_planes in ((blk != 0, 0, False), (blk == 0, 0, True), (blk != nb - 1, 1, False)):
            @pl.when(when)
            def _(side=side, with_planes=with_planes):
                for c in range(2):
                    rows_from(side, h, c, with_planes).wait_recv()

        def tile(dev, piece, j):
            return recv_a[h, dev, piece * gw : (piece + 1) * gw, j * lanes : (j + 1) * lanes]

        for dev in range(0, PARTS, 2):
            for j in range(wx // 2):
                for z in range(depth):
                    for half, value in enumerate(merged(tile(dev, z, j), tile(dev + 1, z, j))):
                        at = (dev // 2) * wx + 2 * j + half
                        left[z * gw : (z + 1) * gw, (at + 1) * lanes : (at + 2) * lanes] = value.astype(BF16)

        def spread_row(x, value):
            for b in range(3):
                shifted = value if b == 1 else pltpu.roll(value, 1 if b == 2 else lanes - 1, 1)
                shifted = shifted.astype(BF16)
                for a in range(3):
                    u = x + a - 1
                    if 0 <= u < rows_x or (u == -1 and a == 0):
                        where = slice((u + 1) * lanes, (u + 2) * lanes)
                        tap = a * 3 + b
                        if tap < 8:
                            right[tap * gw : (tap + 1) * gw, where] = shifted
                        else:
                            for n in range(depth):
                                right[wide + n * gw : wide + (n + 1) * gw, where] = shifted

        def halo_row(side, piece):
            part = slice(piece * gw, (piece + 1) * gw)
            return merged(row_halo[h, side, 0, part], row_halo[h, side, 1, part])[1 - side]

        for z in range(depth):
            left[z * gw : (z + 1) * gw, 0:lanes] = jnp.where(blk == 0, halo_row(0, z), 0.0).astype(BF16)
        spread_row(-1, halo_row(0, depth))
        spread_row(rows_x, jnp.where(blk == nb - 1, 0.0, halo_row(1, depth)))
        for dev in range(0, PARTS, 2):
            for j in range(wx // 2):
                for half, value in enumerate(merged(tile(dev, depth, j), tile(dev + 1, depth, j))):
                    spread_row((dev // 2) * wx + 2 * j + half, value)
        full = lax.dot_general(left[...], right[...], (((1,), (1,)), ((), ())), preferred_element_type=F32)
        main, last = full[:, 0:wide], full[:, wide : 2 * wide]
        tail = main[depth * gw :]
        for z in range(depth):
            tail = jnp.where(jnp.logical_and(lane >= z * gw, lane < (z + 1) * gw), last[z * gw : (z + 1) * gw], tail)
        recv_b[h, blk, 0 : depth * gw, :] = main[0 : depth * gw]
        recv_b[h, blk, depth * gw :, :] = tail

    def b_copy(h, k):
        return remote(
            recv_b.at[h, blk], recv_b.at[h, blk], b_send.at[h, k - 1], b_recv.at[h, k - 1], device(lax.rem(blk + k, nb), me)
        )

    @pl.when(owns)
    def _():
        for h in range(PIECES):
            gradient_part(h)
            for k in range(1, nb):
                b_copy(h, k).start()
        pl.semaphore_signal(go, inc=1, device_id=(gx - 1, gy), device_id_type=MESH)

    @pl.when(jnp.logical_not(owns))
    def _():
        pl.semaphore_wait(go, 1)

    for copy in halo_copies:
        copy.start()

    def c_copy(h, k):
        g = h * OWNERS + mine
        return remote(
            recv_c.at[g], recv_c.at[g], c_send.at[h, k - 1], c_recv.at[g], device(blk, lax.rem(me + k, PARTS))
        )

    @pl.when(owns)
    def _():
        for h in range(PIECES):
            for k in range(1, nb):
                b_copy(h, k).wait_recv()
            total = recv_b[h, 0]
            for k in range(1, nb):
                total = total + recv_b[h, k]
            g = h * OWNERS + mine
            recv_c[g] = pltpu.roll(total * scale, g * gw, 1)
            for k in range(1, PARTS):
                c_copy(h, k).start()

    whole_row = lax.broadcasted_iota(jnp.int32, (wy, ch), 0)

    def views(target, row, value, before, after):
        value32 = value.astype(F32)
        here = slice(row * wy, (row + 1) * wy)
        target[here, ch : 2 * ch] = value
        target[here, 0:ch] = jnp.where(whole_row == 0, before, pltpu.roll(value32, 1, 0)).astype(BF16)
        target[here, 2 * ch : 3 * ch] = jnp.where(whole_row == wy - 1, after, pltpu.roll(value32, wy - 1, 0)).astype(BF16)

    def side_of(row):
        if row == 0:
            return 0, wx - 1
        if row == wx + 1:
            return 2, 0
        return 1, row - 1

    for copy in halo_copies:
        copy.wait_recv()
    halo32 = [[edge_halo[s, o].astype(F32) for o in range(3)] for s in range(2)]
    for row in range(wx + 2):
        origin, x = side_of(row)
        value = cot_halo[0] if row == 0 else cot_halo[1] if row == wx + 1 else cot[x]
        n = depth * wx + x
        views(cot_views, row, value, halo32[0][origin][n : n + 1], halo32[1][origin][n : n + 1])
        for z in range(depth):
            value = planes_halo[0, z] if row == 0 else planes_halo[1, z] if row == wx + 1 else planes[z, x]
            n = z * wx + x
            views(planes_views.at[z], row, value, halo32[0][origin][n : n + 1], halo32[1][origin][n : n + 1])
    forward = jnp.zeros((cells, ch), F32)
    for z in range(depth):
        for a in range(3):
            forward = forward + jnp.dot(
                planes_views[z, a * wy : a * wy + cells, :], weights[z, a], preferred_element_type=F32
            )
    out_ref[...] = (forward + bias[...]).astype(BF16).reshape(wx, wy, ch)
    slopes = jnp.zeros((cells, depth * ch), F32)
    for a in range(3):
        slopes = slopes + lax.dot_general(
            cot_views[(2 - a) * wy : (2 - a) * wy + cells, :],
            weights_back[a],
            (((1,), (1,)), ((), ())),
            preferred_element_type=F32,
        )
    for z in range(depth):
        grad_ref[z] = slopes[:, z * ch : (z + 1) * ch].astype(BF16).reshape(wx, wy, ch)

    for h in range(PIECES):
        for q in range(OWNERS):
            @pl.when(jnp.logical_not(jnp.logical_and(owns, mine == q)))
            def _(h=h, q=q):
                g = h * OWNERS + q
                remote(recv_c.at[g], recv_c.at[g], c_send.at[h, 0], c_recv.at[g], device(blk, 0)).wait_recv()

    slot = lane // gw

    def gathered(rows, shift):
        value = recv_c[(GROUPS - shift) % GROUPS, rows]
        for s in range(1, GROUPS):
            value = jnp.where(slot == s, recv_c[(s - shift) % GROUPS, rows], value)
        return value if shift == 0 else pltpu.roll(value, wide - shift * gw, 1)

    for z in range(depth):
        for tap in range(9):
            at = (z * 9 + tap) * gw
            if tap < 8:
                sums_ref[at : at + gw, :] = gathered(slice(z * gw, (z + 1) * gw), tap)
            else:
                sums_ref[at : at + gw, :] = gathered(slice(depth * gw, (depth + 1) * gw), z)
    at = depth * 9 * gw
    sums_ref[at : at + gw, :] = gathered(slice(depth * gw, (depth + 1) * gw), 4)

    for copy in halo_copies:
        copy.wait_send()
    for when, side, with_planes in row_roles:
        @pl.when(when)
        def _(side=side, with_planes=with_planes):
            for h in range(PIECES):
                for q in range(OWNERS):
                    row_copy(side, h, q, with_planes).wait_send()

    @pl.when(owns)
    def _():
        for h in range(PIECES):
            for k in range(1, OWNERS):
                slab_copy(h, lax.rem(mine + k, OWNERS)).wait_send()
            for k in range(1, nb):
                b_copy(h, k).wait_send()
            for k in range(1, PARTS):
                c_copy(h, k).wait_send()

    @pl.when(jnp.logical_not(owns))
    def _():
        for h in range(PIECES):
            for q in range(OWNERS):
                slab_copy(h, q).wait_send()


def place_body(out_from, grad_from, sums, out_to, grad_to, kernel_to, bias_to, sem):
    base = kernel_to.shape[0]
    copies = [
        pltpu.make_async_copy(grad_from, grad_to, sem.at[0]),
        pltpu.make_async_copy(sums.at[0:base], kernel_to, sem.at[1]),
        pltpu.make_async_copy(out_from, out_to, sem.at[2]),
        pltpu.make_async_copy(sums.at[base : base + 1], bias_to, sem.at[3]),
    ]
    for copy in copies:
        copy.start()
    for copy in copies:
        copy.wait()


def by_part(nx, ny, planes, kernel, bias, cotangent):
    depth, wx, wy, ch = planes.shape
    cells = wx * wy
    gw = ch // GROUPS
    nb = (nx // LOW_X) * (ny // LOW_Y)
    needed = depth * 9 * gw + 8
    chunk = -(-needed // (PARTS * 8)) * 8
    scale = np.float32(1.0) / np.sqrt(np.float32(cells * nx * ny))
    dma = pltpu.SemaphoreType.DMA
    vmem = pl.BlockSpec(memory_space=pltpu.VMEM)
    hbm = pl.BlockSpec(memory_space=pltpu.HBM)
    out, grad, sums = pl.pallas_call(
        functools.partial(kernel_body, nx, ny, scale, chunk),
        out_shape=(
            jax.ShapeDtypeStruct((wx, wy, ch), BF16),
            jax.ShapeDtypeStruct((depth, wx, wy, ch), BF16),
            jax.ShapeDtypeStruct((PARTS, chunk, ch), F32),
        ),
        in_specs=[hbm, hbm, hbm, hbm],
        out_specs=(vmem,) * 3,
        scratch_shapes=[
            pltpu.VMEM((depth, wx, wy, ch), BF16),
            pltpu.VMEM((depth, 3, 3, gw, ch), BF16),
            pltpu.VMEM((1, ch), F32),
            pltpu.VMEM((wx, wy, ch), BF16),
            pltpu.VMEM((2, 16, ch), BF16),
            pltpu.VMEM((2, 3, 16, ch), BF16),
            pltpu.VMEM((2, wy, ch), BF16),
            pltpu.VMEM((2, depth, wy, ch), BF16),
            pltpu.VMEM((depth, 3, 3 * ch, ch), BF16),
            pltpu.VMEM((3, depth * ch, 3 * ch), BF16),
            pltpu.VMEM((depth * ch, cells), BF16),
            pltpu.VMEM(((wx + 2) * wy, 3 * ch), BF16),
            pltpu.VMEM((depth, (wx + 2) * wy, 3 * ch), BF16),
            pltpu.VMEM((PARTS, chunk, ch), F32),
            pltpu.VMEM((PARTS - 1, chunk, ch), F32),
            pltpu.VMEM((nb, chunk, ch), F32),
            dma((4,)), dma((10,)), dma((10,)),
            dma((2, PARTS - 1)), dma((2, PARTS - 1)),
            dma((2, max(nb - 1, 1))), dma((2, max(nb - 1, 1))),
            dma((2, PARTS - 1)), dma((2, PARTS - 1)),
        ],
        compiler_params=pltpu.CompilerParams(
            collective_id=0, has_side_effects=True, vmem_limit_bytes=32 * 1024 * 1024
        ),
    )(*(pltpu.with_memory_space_constraint(x, pltpu.HBM) for x in (planes, kernel, bias.reshape(1, ch), cotangent)))
    return out, grad, sums.reshape(PARTS * chunk, ch)


def by_owner(nx, planes, kernel, bias, cotangent):
    depth, wx, wy, ch = planes.shape
    cells = wx * wy
    gw = ch // GROUPS
    lanes = 2 * wy
    nb = nx // LOW_X
    scale = np.float32(1.0) / np.sqrt(np.float32(cells * nx * 2))
    dma = pltpu.SemaphoreType.DMA
    vmem = pl.BlockSpec(memory_space=pltpu.VMEM)
    hbm = pl.BlockSpec(memory_space=pltpu.HBM)
    return pl.pallas_call(
        functools.partial(owner_body, nx, scale),
        out_shape=(
            jax.ShapeDtypeStruct((wx, wy, ch), BF16),
            jax.ShapeDtypeStruct((depth, wx, wy, ch), BF16),
            jax.ShapeDtypeStruct((depth * 9 * gw + gw, ch), F32),
        ),
        in_specs=[hbm, hbm, hbm, hbm],
        out_specs=(vmem,) * 3,
        scratch_shapes=[
            pltpu.VMEM((depth, wx, wy, ch), BF16),
            pltpu.VMEM((depth, 3, 3, gw, ch), BF16),
            pltpu.VMEM((1, ch), F32),
            pltpu.VMEM((wx, wy, ch), BF16),
            pltpu.VMEM((2, 16, ch), BF16),
            pltpu.VMEM((2, 3, 16, ch), BF16),
            pltpu.VMEM((2, wy, ch), BF16),
            pltpu.VMEM((2, depth, wy, ch), BF16),
            pltpu.VMEM((depth, 3, 3 * ch, ch), BF16),
            pltpu.VMEM((3, depth * ch, 3 * ch), BF16),
            pltpu.VMEM(((wx + 2) * wy, 3 * ch), BF16),
            pltpu.VMEM((depth, (wx + 2) * wy, 3 * ch), BF16),
            pltpu.VMEM((GROUPS, (depth + 1) * gw, cells), BF16),
            pltpu.VMEM((PIECES, PARTS, (depth + 1) * gw, cells), BF16),
            pltpu.VMEM((PIECES, 2, 2, (depth + 1) * gw, lanes), BF16),
            pltpu.VMEM(((depth + 1) * gw, (LOW_X * wx + 1) * lanes), BF16),
            pltpu.VMEM((2 * ch, (LOW_X * wx + 1) * lanes), BF16),
            pltpu.VMEM((PIECES, nb, (depth + 1) * gw, ch), F32),
            pltpu.VMEM((GROUPS, (depth + 1) * gw, ch), F32),
            dma((3 + depth,)), dma((10,)), dma((10,)),
            dma((PIECES, OWNERS)), dma((PIECES, PARTS)),
            dma((PIECES, OWNERS)), dma((PIECES, 2, 2)),
            dma((PIECES, nb - 1)), dma((PIECES, nb - 1)),
            dma((PIECES, PARTS - 1)), dma((GROUPS,)),
            pltpu.SemaphoreType.REGULAR,
        ],
        compiler_params=pltpu.CompilerParams(
            collective_id=0, has_side_effects=True, vmem_limit_bytes=32 * 1024 * 1024
        ),
    )(*(pltpu.with_memory_space_constraint(x, pltpu.HBM) for x in (planes, kernel, bias.reshape(1, ch), cotangent)))


def shards(nx, ny, planes, kernel, bias, cotangent):
    depth, wx, wy, ch = planes.shape
    gw = ch // GROUPS
    if ny == 2 and nx == 4 * LOW_X and (depth, wx, 2 * wy, ch, gw) == (3, 4, 128, 128, 16):
        out, grad, sums = by_owner(nx, planes, kernel, bias, cotangent)
    else:
        out, grad, sums = by_part(nx, ny, planes, kernel, bias, cotangent)
    dma = pltpu.SemaphoreType.DMA
    vmem = pl.BlockSpec(memory_space=pltpu.VMEM)
    hbm = pl.BlockSpec(memory_space=pltpu.HBM)
    base = depth * 9 * gw
    out, grad, kernel_grad, bias_grad = pl.pallas_call(
        place_body,
        out_shape=(
            jax.ShapeDtypeStruct(out.shape, BF16),
            jax.ShapeDtypeStruct(grad.shape, BF16),
            jax.ShapeDtypeStruct((base, ch), F32),
            jax.ShapeDtypeStruct((1, ch), F32),
        ),
        in_specs=[vmem] * 3,
        out_specs=(hbm, hbm, hbm, hbm),
        scratch_shapes=[dma((4,))],
    )(*(pltpu.with_memory_space_constraint(x, pltpu.VMEM) for x in (out, grad, sums)))
    return out, grad, kernel_grad.reshape(kernel.shape), bias_grad.reshape(ch)


def solution(mesh):
    in_specs = (P(None, "gx", "gy", None), P(), P(), P("gx", "gy", None))
    out_specs = (P("gx", "gy", None), P(None, "gx", "gy", None), P(), P())
    body = functools.partial(shards, mesh.shape["gx"], mesh.shape["gy"])
    return jax.shard_map(body, mesh=mesh, in_specs=in_specs, out_specs=out_specs, check_vma=False)
```

```python
import functools

import jax
import jax.numpy as jnp
import numpy as np
from jax import lax
from jax.experimental import pallas as pl
from jax.experimental.pallas import tpu as pltpu
from jax.sharding import PartitionSpec as P

GROUPS = 8
MESH = pl.DeviceIdType.MESH
LOW_X = 4
LOW_Y = 2
PARTS = LOW_X * LOW_Y
OWNERS = PARTS // 2
PIECES = GROUPS // OWNERS
F32 = jnp.float32
BF16 = jnp.bfloat16


def kernel_body(
    nx, ny, scale, chunk,
    planes_hbm, kernel_hbm, bias_hbm, cot_hbm,
    out_ref, grad_ref, sums_ref,
    planes, taps, bias, cot, edges, edge_halo, cot_halo, planes_halo,
    weights, weights_back, planes_t, cot_views, planes_views,
    part, recv_a, recv_b,
    local_sem, halo_send, halo_recv, a_send, a_recv, b_send, b_recv, c_send, c_recv,
):
    depth, wx, wy, ch = planes.shape
    cells = wx * wy
    gw = ch // GROUPS
    gx = lax.axis_index("gx")
    gy = lax.axis_index("gy")
    nb = (nx // LOW_X) * (ny // LOW_Y)
    high_y = ny // LOW_Y
    low_gx, low_gy = lax.rem(gx, LOW_X), lax.rem(gy, LOW_Y)
    high_gx, high_gy = lax.div(gx, LOW_X), lax.div(gy, LOW_Y)
    ia = low_gx * LOW_Y + low_gy
    ib = high_gx * high_y + high_gy
    peers_a = [None]
    for k in range(1, PARTS):
        j = lax.rem(ia + k, PARTS)
        peers_a.append((j, (high_gx * LOW_X + lax.div(j, LOW_Y), high_gy * LOW_Y + lax.rem(j, LOW_Y))))
    peers_b = [None]
    for k in range(1, nb):
        j = lax.rem(ib + k, nb)
        peers_b.append((lax.div(j, high_y) * LOW_X + low_gx, lax.rem(j, high_y) * LOW_Y + low_gy))
    around_x = {-1: lax.rem(gx + nx - 1, nx), 0: gx, 1: lax.rem(gx + 1, nx)}
    around_y = {-1: lax.rem(gy + ny - 1, ny), 0: gy, 1: lax.rem(gy + 1, ny)}

    def peer_a(k):
        return peers_a[k]

    def peer_b(k):
        return peers_b[k]

    def near(dx, dy):
        return (around_x[dx], around_y[dy])

    partners = [peer_a(k)[1] for k in range(1, PARTS)] + [peer_b(k) for k in range(1, nb)]
    for dy in ((0, 1) if ny == 2 else (-1, 0, 1)):
        for dx in (-1, 0, 1):
            if (dx, dy) != (0, 0):
                partners.append(near(dx, dy))
    in_cot = pltpu.make_async_copy(cot_hbm, cot, local_sem.at[0])
    in_planes = pltpu.make_async_copy(planes_hbm, planes, local_sem.at[1])
    in_taps = pltpu.make_async_copy(kernel_hbm, taps, local_sem.at[2])
    in_cot.start()
    in_planes.start()
    in_taps.start()
    in_bias = pltpu.make_async_copy(bias_hbm, bias, local_sem.at[3])
    in_bias.start()
    barrier = pltpu.get_barrier_semaphore()
    for where in partners:
        pl.semaphore_signal(barrier, inc=1, device_id=where, device_id_type=MESH)

    in_cot.wait()
    in_planes.wait()

    rows = [(planes, (z, x)) for z in range(depth) for x in range(wx)] + [(cot, (x,)) for x in range(wx)]
    lane_row = lax.broadcasted_iota(jnp.int32, (16, ch), 0)
    low = jnp.zeros((16, ch), F32)
    high = jnp.zeros((16, ch), F32)
    for r, (ref, at) in enumerate(rows):
        first = ref[at + (slice(0, 16),)].astype(F32)[0:1]
        last = ref[at + (slice(wy - 16, wy),)].astype(F32)[15:16]
        low = jnp.where(lane_row == r, first, low)
        high = jnp.where(lane_row == r, last, high)
    edges[0] = low.astype(BF16)
    edges[1] = high.astype(BF16)

    pl.semaphore_wait(barrier, len(partners))

    def remote(src, dst, send, recv, where):
        copy = pltpu.make_async_remote_copy(
            src_ref=src, dst_ref=dst, send_sem=send, recv_sem=recv, device_id=where, device_id_type=MESH
        )
        copy.start()
        return copy

    cot_copies = [
        remote(cot.at[0], cot_halo.at[1], halo_send.at[0], halo_recv.at[0], near(-1, 0)),
        remote(cot.at[wx - 1], cot_halo.at[0], halo_send.at[1], halo_recv.at[1], near(1, 0)),
    ]
    number = 2
    for side, dy in ((1, -1), (0, 1)):
        for dx in (-1, 0, 1):
            cot_copies.append(
                remote(edges.at[1 - side], edge_halo.at[side, 1 - dx], halo_send.at[number], halo_recv.at[number], near(dx, dy))
            )
            number += 1
    planes_copies = [
        remote(planes.at[:, 0], planes_halo.at[1], halo_send.at[8], halo_recv.at[8], near(-1, 0)),
        remote(planes.at[:, wx - 1], planes_halo.at[0], halo_send.at[9], halo_recv.at[9], near(1, 0)),
    ]

    row_group = lax.broadcasted_iota(jnp.int32, (ch, ch), 0) // gw
    col_group = lax.broadcasted_iota(jnp.int32, (ch, ch), 1) // gw
    mask = row_group == col_group
    mask_w = jnp.where(mask, 1.0, 0.0).astype(BF16)
    for z in range(depth):
        planes_t[z * ch : (z + 1) * ch, :] = planes[z].reshape(cells, ch).astype(F32).T.astype(BF16)
    spread = jnp.sum(cot[...].reshape(cells, ch).astype(F32), axis=0, keepdims=True)
    whole_row = lax.broadcasted_iota(jnp.int32, (wy, ch), 0)

    def views(target, row, value, left, right):
        value32 = value.astype(F32)
        here = slice(row * wy, (row + 1) * wy)
        target[here, ch : 2 * ch] = value
        target[here, 0:ch] = jnp.where(whole_row == 0, left, pltpu.roll(value32, 1, 0)).astype(BF16)
        target[here, 2 * ch : 3 * ch] = jnp.where(whole_row == wy - 1, right, pltpu.roll(value32, wy - 1, 0)).astype(BF16)

    def side_of(row):
        if row == 0:
            return 0, wx - 1
        if row == wx + 1:
            return 2, 0
        return 1, row - 1

    for copy in cot_copies:
        copy.wait_recv()
    halo32 = [[edge_halo[s, o].astype(F32) for o in range(3)] for s in range(2)]
    for row in range(wx + 2):
        origin, x = side_of(row)
        value = cot_halo[0] if row == 0 else cot_halo[1] if row == wx + 1 else cot[x]
        r = depth * wx + x
        views(cot_views, row, value, halo32[0][origin][r : r + 1], halo32[1][origin][r : r + 1])

    def put(row, value):
        part[row // chunk, row % chunk : row % chunk + 8, :] = value

    for a in range(3):
        full = jnp.dot(
            planes_t[...], cot_views[(2 - a) * wy : (2 - a) * wy + cells, :], preferred_element_type=F32
        )
        for z in range(depth):
            for b in range(3):
                block = full[z * ch : (z + 1) * ch, (2 - b) * ch : (3 - b) * ch]
                block = jnp.where(mask, block, 0.0).reshape(GROUPS, gw, ch).sum(axis=0)
                start = ((z * 3 + a) * 3 + b) * gw
                put(start, block[0:8])
                put(start + 8, block[8:16])
    base = depth * 9 * gw
    put(base, jnp.broadcast_to(spread, (8, ch)))
    for row in range(base + 8, PARTS * chunk, 8):
        put(row, jnp.zeros((8, ch), F32))

    pieces = [slice(0, 32), slice(32, chunk)]
    a_copies = [[], []]
    for h, rows in enumerate(pieces):
        for k in range(1, PARTS):
            j, where = peer_a(k)
            a_copies[h].append(
                remote(part.at[j, rows], recv_a.at[k - 1, rows], a_send.at[h, k - 1], a_recv.at[h, k - 1], where)
            )

    in_taps.wait()
    in_bias.wait()
    for z in range(depth):
        for a in range(3):
            for b in range(3):
                tile = jnp.concatenate([taps[z, a, b]] * GROUPS, axis=0) * mask_w
                weights[z, a, b * ch : (b + 1) * ch, :] = tile
                weights_back[a, z * ch : (z + 1) * ch, (2 - b) * ch : (3 - b) * ch] = tile
    for copy in planes_copies:
        copy.wait_recv()
    for z in range(depth):
        for row in range(wx + 2):
            origin, x = side_of(row)
            value = planes_halo[0, z] if row == 0 else planes_halo[1, z] if row == wx + 1 else planes[z, x]
            r = z * wx + x
            views(planes_views.at[z], row, value, halo32[0][origin][r : r + 1], halo32[1][origin][r : r + 1])
    forward = jnp.zeros((cells, ch), F32)
    for z in range(depth):
        for a in range(3):
            forward = forward + jnp.dot(
                planes_views[z, a * wy : a * wy + cells, :], weights[z, a], preferred_element_type=F32
            )
    out_ref[...] = (forward + bias[...]).astype(BF16).reshape(wx, wy, ch)

    b_copies = [[], []]
    for h, rows in enumerate(pieces):
        for copy in a_copies[h]:
            copy.wait_recv()
        reduced = part[ia, rows]
        for k in range(PARTS - 1):
            reduced = reduced + recv_a[k, rows]
        recv_b[ib, rows] = reduced
        for k in range(1, nb):
            b_copies[h].append(
                remote(recv_b.at[ib, rows], recv_b.at[ib, rows], b_send.at[h, k - 1], b_recv.at[h, k - 1], peer_b(k))
            )

    slopes = jnp.zeros((cells, depth * ch), F32)
    for a in range(3):
        slopes = slopes + lax.dot_general(
            cot_views[(2 - a) * wy : (2 - a) * wy + cells, :],
            weights_back[a],
            (((1,), (1,)), ((), ())),
            preferred_element_type=F32,
        )
    for z in range(depth):
        grad_ref[z] = slopes[:, z * ch : (z + 1) * ch].astype(BF16).reshape(wx, wy, ch)

    c_copies = []
    for h, rows in enumerate(pieces):
        for copy in b_copies[h]:
            copy.wait_recv()
        value = recv_b[0, rows]
        for k in range(1, nb):
            value = value + recv_b[k, rows]
        sums_ref[ia, rows] = value * scale
        for k in range(1, PARTS):
            _, where = peer_a(k)
            c_copies.append(
                remote(sums_ref.at[ia, rows], sums_ref.at[ia, rows], c_send.at[h, k - 1], c_recv.at[h, k - 1], where)
            )

    for copy in cot_copies + planes_copies + sum(a_copies + b_copies, []):
        copy.wait_send()
    for copy in c_copies:
        copy.wait()

def owner_body(
    nx, scale,
    planes_hbm, kernel_hbm, bias_hbm, cot_hbm,
    out_ref, grad_ref, sums_ref,
    planes, taps, bias, cot, edges, edge_halo, cot_halo, planes_halo,
    weights, weights_back, cot_views, planes_views,
    slabs, recv_a, row_halo, left, right, recv_b, recv_c,
    local_sem, halo_send, halo_recv, a_send, a_recv, z_send, z_recv, b_send, b_recv, c_send, c_recv, go,
):
    depth, wx, wy, ch = planes.shape
    cells = wx * wy
    gw = ch // GROUPS
    lanes = 2 * wy
    rows_x = LOW_X * wx
    nb = nx // LOW_X
    gx = lax.axis_index("gx")
    gy = lax.axis_index("gy")
    blk, r = lax.div(gx, LOW_X), lax.rem(gx, LOW_X)
    me = r * 2 + gy
    owns = lax.rem(r, 2) == 1
    mine = lax.div(r, 2) * 2 + gy
    above, below = lax.rem(blk + 1, nb), lax.rem(blk + nb - 1, nb)

    def device(block, index):
        return (block * LOW_X + lax.div(index, 2), lax.rem(index, 2))

    def owner(block, q):
        return (block * LOW_X + 2 * lax.div(q, 2) + 1, lax.rem(q, 2))

    around_x = {-1: lax.rem(gx + nx - 1, nx), 0: gx, 1: lax.rem(gx + 1, nx)}

    def near(dx, dy):
        return (around_x[dx], lax.rem(gy + dy + 2, 2))

    in_cot = pltpu.make_async_copy(cot_hbm, cot, local_sem.at[0])
    in_planes = [pltpu.make_async_copy(planes_hbm.at[z], planes.at[z], local_sem.at[1 + z]) for z in range(depth)]
    in_taps = pltpu.make_async_copy(kernel_hbm, taps, local_sem.at[1 + depth])
    in_bias = pltpu.make_async_copy(bias_hbm, bias, local_sem.at[2 + depth])
    in_cot.start()
    for copy in in_planes:
        copy.start()
    in_taps.start()
    in_bias.start()
    barrier = pltpu.get_barrier_semaphore()

    def greet(where):
        pl.semaphore_signal(barrier, inc=1, device_id=where, device_id_type=MESH)

    @pl.when(owns)
    def _():
        for k in range(1, PARTS):
            greet(device(blk, lax.rem(me + k, PARTS)))
        for c in range(2):
            greet(device(below, PARTS - 2 + c))

        @pl.when(blk != nb - 1)
        def _():
            for c in range(2):
                greet(device(above, c))

        @pl.when(blk != 1)
        def _():
            for c in range(2):
                greet(device(below, c))

        @pl.when(blk == 1)
        def _():
            for c in range(2):
                greet(device(nb - 1, PARTS - 2 + c))

    @pl.when(jnp.logical_and(r == 0, blk == 0))
    def _():
        for c in range(2):
            greet(device(nb - 1, PARTS - 2 + c))

    in_cot.wait()
    slabs[:, depth * gw :, :] = cot[...].reshape(cells, ch).astype(F32).T.astype(BF16).reshape(GROUPS, gw, cells)
    for z in range(depth):
        in_planes[z].wait()
        slabs[:, z * gw : (z + 1) * gw, :] = planes[z].reshape(cells, ch).astype(F32).T.astype(BF16).reshape(GROUPS, gw, cells)

    pl.semaphore_wait(
        barrier,
        jnp.where(owns, OWNERS - 1, OWNERS)
        + jnp.where(jnp.logical_and(r == 0, blk != 0), 2 * OWNERS, 0)
        + jnp.where(r == LOW_X - 1, jnp.where(blk == nb - 1, 2 * OWNERS + 2, OWNERS), 0),

    )

    def remote(src, dst, send, recv, where):
        return pltpu.make_async_remote_copy(
            src_ref=src, dst_ref=dst, send_sem=send, recv_sem=recv, device_id=where, device_id_type=MESH
        )

    def row_copy(side, h, q, with_planes=False):
        rows = slice(0 if with_planes else depth * gw, (depth + 1) * gw)
        cols = slice((1 - side) * (cells - lanes), (1 - side) * (cells - lanes) + lanes)
        return remote(
            slabs.at[h * OWNERS + q, rows, cols], row_halo.at[h, side, gy, rows],
            z_send.at[h, q], z_recv.at[h, side, gy], owner((above, below)[side], q),
        )

    def rows_from(side, h, c, with_planes=False):
        rows = slice(0 if with_planes else depth * gw, (depth + 1) * gw)
        return remote(
            slabs.at[0, rows, 0:lanes], row_halo.at[h, side, c, rows], z_send.at[h, 0], z_recv.at[h, side, c], device(blk, c)
        )

    up = jnp.logical_and(r == LOW_X - 1, blk != nb - 1)
    seam = jnp.logical_and(r == LOW_X - 1, blk == nb - 1)
    down = jnp.logical_and(r == 0, blk != 0)
    row_roles = ((up, 0, False), (seam, 0, True), (down, 1, False))

    def slab_copy(h, q):
        return remote(slabs.at[h * OWNERS + q], recv_a.at[h, me], a_send.at[h, q], a_recv.at[h, me], owner(blk, q))

    def own_slab(h):
        return pltpu.make_async_copy(slabs.at[h * OWNERS + mine], recv_a.at[h, me], a_recv.at[h, me])

    for h in range(PIECES):
        @pl.when(owns)
        def _(h=h):
            for k in range(1, OWNERS):
                slab_copy(h, lax.rem(mine + k, OWNERS)).start()
            own_slab(h).start()

        @pl.when(jnp.logical_not(owns))
        def _(h=h):
            for q in range(OWNERS):
                slab_copy(h, q).start()

        for when, side, with_planes in row_roles:
            @pl.when(when)
            def _(h=h, side=side, with_planes=with_planes):
                for q in range(OWNERS):
                    row_copy(side, h, q, with_planes).start()

    rows = [(planes, (z, x)) for z in range(depth) for x in range(wx)] + [(cot, (x,)) for x in range(wx)]
    lane_row = lax.broadcasted_iota(jnp.int32, (16, ch), 0)
    low = jnp.zeros((16, ch), F32)
    high = jnp.zeros((16, ch), F32)
    for n, (ref, at) in enumerate(rows):
        first = ref[at + (slice(0, 16),)].astype(F32)[0:1]
        last = ref[at + (slice(wy - 16, wy),)].astype(F32)[15:16]
        low = jnp.where(lane_row == n, first, low)
        high = jnp.where(lane_row == n, last, high)
    edges[0] = low.astype(BF16)
    edges[1] = high.astype(BF16)

    halo_copies = [
        remote(cot.at[0], cot_halo.at[1], halo_send.at[0], halo_recv.at[0], near(-1, 0)),
        remote(cot.at[wx - 1], cot_halo.at[0], halo_send.at[1], halo_recv.at[1], near(1, 0)),
        remote(planes.at[:, 0], planes_halo.at[1], halo_send.at[8], halo_recv.at[8], near(-1, 0)),
        remote(planes.at[:, wx - 1], planes_halo.at[0], halo_send.at[9], halo_recv.at[9], near(1, 0)),
    ]
    number = 2
    for side, dy in ((1, -1), (0, 1)):
        for dx in (-1, 0, 1):
            halo_copies.append(
                remote(edges.at[1 - side], edge_halo.at[side, 1 - dx], halo_send.at[number], halo_recv.at[number], near(dx, dy))
            )
            number += 1
    row_group = lax.broadcasted_iota(jnp.int32, (ch, ch), 0) // gw
    col_group = lax.broadcasted_iota(jnp.int32, (ch, ch), 1) // gw
    mask_w = jnp.where(row_group == col_group, 1.0, 0.0).astype(BF16)
    in_taps.wait()
    in_bias.wait()
    for z in range(depth):
        for a in range(3):
            for b in range(3):
                tile = jnp.concatenate([taps[z, a, b]] * GROUPS, axis=0) * mask_w
                weights[z, a, b * ch : (b + 1) * ch, :] = tile
                weights_back[a, z * ch : (z + 1) * ch, (2 - b) * ch : (3 - b) * ch] = tile

    wide = GROUPS * gw
    lane = lax.broadcasted_iota(jnp.int32, (gw, lanes), 1)
    first_half = lane < wy
    slot8 = lax.broadcasted_iota(jnp.int32, (8, lanes), 1) // gw
    nothing = jnp.zeros((gw, lanes), BF16)

    @pl.when(owns)
    def _():
        left[depth * gw :, :] = jnp.ones((gw, left.shape[1]), BF16)
        right[wide + 2 * depth * gw :, :] = jnp.zeros((right.shape[0] - wide - 2 * depth * gw, right.shape[1]), BF16)
        right[3 * gw :, 0:lanes] = jnp.zeros((right.shape[0] - 3 * gw, lanes), BF16)

    def merged(g0, g1):
        return (
            jnp.where(first_half, g0, pltpu.roll(g1, wy, 1)),
            jnp.where(first_half, pltpu.roll(g0, wy, 1), g1),
        )

    def arrive(h):
        for src in range(PARTS):
            remote(slabs.at[0], recv_a.at[h, src], a_send.at[h, 0], a_recv.at[h, src], device(blk, src)).wait_recv()
        for when, side, with_planes in ((blk != 0, 0, False), (blk == 0, 0, True), (blk != nb - 1, 1, False)):
            @pl.when(when)
            def _(side=side, with_planes=with_planes):
                for c in range(2):
                    rows_from(side, h, c, with_planes).wait_recv()

    def gradient_part(h):
        def tile(dev, piece, j):
            return recv_a[h, dev, piece * gw : (piece + 1) * gw, j * lanes : (j + 1) * lanes]

        for dev in range(0, PARTS, 2):
            for j in range(wx // 2):
                for z in range(depth):
                    for half, value in enumerate(merged(tile(dev, z, j), tile(dev + 1, z, j))):
                        at = (dev // 2) * wx + 2 * j + half
                        left[z * gw : (z + 1) * gw, (at + 1) * lanes : (at + 2) * lanes] = value

        def spread_row(x, value):
            for b in range(3):
                shifted = value if b == 1 else pltpu.roll(value, 1 if b == 2 else lanes - 1, 1)
                for a in range(3):
                    u = x + a - 1
                    if 0 <= u < rows_x or (u == -1 and a == 0):
                        where = slice((u + 1) * lanes, (u + 2) * lanes)
                        tap = a * 3 + b
                        if tap < 8:
                            right[tap * gw : (tap + 1) * gw, where] = shifted
                        else:
                            for n in range(2 * depth):
                                right[wide + n * gw : wide + (n + 1) * gw, where] = shifted

        def halo_row(side, piece):
            part = slice(piece * gw, (piece + 1) * gw)
            return merged(row_halo[h, side, 0, part], row_halo[h, side, 1, part])[1 - side]

        for z in range(depth):
            left[z * gw : (z + 1) * gw, 0:lanes] = jnp.where(blk == 0, halo_row(0, z), nothing)
        spread_row(-1, halo_row(0, depth))
        spread_row(rows_x, jnp.where(blk == nb - 1, nothing, halo_row(1, depth)))
        for dev in range(0, PARTS, 2):
            for j in range(wx // 2):
                for half, value in enumerate(merged(tile(dev, depth, j), tile(dev + 1, depth, j))):
                    spread_row((dev // 2) * wx + 2 * j + half, value)
        full = lax.dot_general(left[...], right[...], (((1,), (1,)), ((), ())), preferred_element_type=F32)
        main, last = full[:, 0:wide], full[:, wide : 2 * wide]
        tail = main[depth * gw :]
        tail = pltpu.roll(tail, 2 * gw, 1)[0:8]
        for n in range(2 * depth):
            z, low_rows = n % depth, n < depth
            rows = last[z * gw : z * gw + 8] if low_rows else last[z * gw + 8 : (z + 1) * gw]
            tail = jnp.where(slot8 == n, rows, tail)
        recv_b[h, blk, 0 : depth * gw, :] = main[0 : depth * gw]
        recv_b[h, blk, depth * gw :, :] = tail

    def b_copy(h, k):
        return remote(
            recv_b.at[h, blk], recv_b.at[h, blk], b_send.at[h, k - 1], b_recv.at[h, k - 1], device(lax.rem(blk + k, nb), me)
        )

    @pl.when(owns)
    def _():
        arrive(0)
        pl.semaphore_signal(go, inc=1, device_id=(gx - 1, gy), device_id_type=MESH)

    @pl.when(jnp.logical_not(owns))
    def _():
        pl.semaphore_wait(go, 1)

    for copy in halo_copies:
        copy.start()

    @pl.when(owns)
    def _():
        for h in range(PIECES):
            if h > 0:
                arrive(h)
            gradient_part(h)
            for k in range(1, nb):
                b_copy(h, k).start()

    def c_copy(h, k):
        g = h * OWNERS + mine
        return remote(
            recv_c.at[g], recv_c.at[g], c_send.at[h, k - 1], c_recv.at[g], device(blk, lax.rem(me + k, PARTS))
        )

    @pl.when(owns)
    def _():
        for h in range(PIECES):
            for k in range(1, nb):
                b_copy(h, k).wait_recv()
            total = recv_b[h, 0]
            for k in range(1, nb):
                total = total + recv_b[h, k]
            g = h * OWNERS + mine
            recv_c[g] = pltpu.roll(total * scale, g * gw, 1)
            for k in range(1, PARTS):
                c_copy(h, k).start()

    whole_row = lax.broadcasted_iota(jnp.int32, (wy, ch), 0)

    def views(target, row, value, before, after):
        value32 = value.astype(F32)
        here = slice(row * wy, (row + 1) * wy)
        target[here, ch : 2 * ch] = value
        target[here, 0:ch] = jnp.where(whole_row == 0, before, pltpu.roll(value32, 1, 0)).astype(BF16)
        target[here, 2 * ch : 3 * ch] = jnp.where(whole_row == wy - 1, after, pltpu.roll(value32, wy - 1, 0)).astype(BF16)

    def side_of(row):
        if row == 0:
            return 0, wx - 1
        if row == wx + 1:
            return 2, 0
        return 1, row - 1

    for copy in halo_copies:
        copy.wait_recv()
    halo32 = [[edge_halo[s, o].astype(F32) for o in range(3)] for s in range(2)]
    for row in range(wx + 2):
        origin, x = side_of(row)
        value = cot_halo[0] if row == 0 else cot_halo[1] if row == wx + 1 else cot[x]
        n = depth * wx + x
        views(cot_views, row, value, halo32[0][origin][n : n + 1], halo32[1][origin][n : n + 1])
        for z in range(depth):
            value = planes_halo[0, z] if row == 0 else planes_halo[1, z] if row == wx + 1 else planes[z, x]
            n = z * wx + x
            views(planes_views.at[z], row, value, halo32[0][origin][n : n + 1], halo32[1][origin][n : n + 1])
    forward = jnp.zeros((cells, ch), F32)
    for z in range(depth):
        for a in range(3):
            forward = forward + jnp.dot(
                planes_views[z, a * wy : a * wy + cells, :], weights[z, a], preferred_element_type=F32
            )
    out_ref[...] = (forward + bias[...]).astype(BF16).reshape(wx, wy, ch)
    slopes = jnp.zeros((cells, depth * ch), F32)
    for a in range(3):
        slopes = slopes + lax.dot_general(
            cot_views[(2 - a) * wy : (2 - a) * wy + cells, :],
            weights_back[a],
            (((1,), (1,)), ((), ())),
            preferred_element_type=F32,
        )
    for z in range(depth):
        grad_ref[z] = slopes[:, z * ch : (z + 1) * ch].astype(BF16).reshape(wx, wy, ch)

    for h in range(PIECES):
        for q in range(OWNERS):
            @pl.when(jnp.logical_not(jnp.logical_and(owns, mine == q)))
            def _(h=h, q=q):
                g = h * OWNERS + q
                remote(recv_c.at[g], recv_c.at[g], c_send.at[h, 0], c_recv.at[g], device(blk, 0)).wait_recv()

    def gathered(rows, shift):
        value = recv_c[(GROUPS - shift) % GROUPS, rows]
        slot = lax.broadcasted_iota(jnp.int32, value.shape, 1) // gw
        for s in range(1, GROUPS):
            value = jnp.where(slot == s, recv_c[(s - shift) % GROUPS, rows], value)
        return value if shift == 0 else pltpu.roll(value, wide - shift * gw, 1)

    tail_rows = slice(depth * gw, depth * gw + 8)
    for z in range(depth):
        for tap in range(9):
            at = (z * 9 + tap) * gw
            if tap < 8:
                sums_ref[at : at + gw, :] = gathered(slice(z * gw, (z + 1) * gw), tap)
            else:
                for n in range(2):
                    sums_ref[at + 8 * n : at + 8 * n + 8, :] = gathered(tail_rows, z + n * depth)
    at = depth * 9 * gw
    sums_ref[at : at + 8, :] = gathered(tail_rows, 2 * depth)

    for copy in halo_copies:
        copy.wait_send()
    for when, side, with_planes in row_roles:
        @pl.when(when)
        def _(side=side, with_planes=with_planes):
            for h in range(PIECES):
                for q in range(OWNERS):
                    row_copy(side, h, q, with_planes).wait_send()

    @pl.when(owns)
    def _():
        for h in range(PIECES):
            for k in range(1, OWNERS):
                slab_copy(h, lax.rem(mine + k, OWNERS)).wait_send()
            for k in range(1, nb):
                b_copy(h, k).wait_send()
            for k in range(1, PARTS):
                c_copy(h, k).wait_send()

    @pl.when(jnp.logical_not(owns))
    def _():
        for h in range(PIECES):
            for q in range(OWNERS):
                slab_copy(h, q).wait_send()


def place_body(out_from, grad_from, sums, out_to, grad_to, kernel_to, bias_to, sem):
    base = kernel_to.shape[0]
    copies = [
        pltpu.make_async_copy(grad_from, grad_to, sem.at[0]),
        pltpu.make_async_copy(sums.at[0:base], kernel_to, sem.at[1]),
        pltpu.make_async_copy(out_from, out_to, sem.at[2]),
        pltpu.make_async_copy(sums.at[base : base + 1], bias_to, sem.at[3]),
    ]
    for copy in copies:
        copy.start()
    for copy in copies:
        copy.wait()


def by_part(nx, ny, planes, kernel, bias, cotangent):
    depth, wx, wy, ch = planes.shape
    cells = wx * wy
    gw = ch // GROUPS
    nb = (nx // LOW_X) * (ny // LOW_Y)
    needed = depth * 9 * gw + 8
    chunk = -(-needed // (PARTS * 8)) * 8
    scale = np.float32(1.0) / np.sqrt(np.float32(cells * nx * ny))
    dma = pltpu.SemaphoreType.DMA
    vmem = pl.BlockSpec(memory_space=pltpu.VMEM)
    hbm = pl.BlockSpec(memory_space=pltpu.HBM)
    out, grad, sums = pl.pallas_call(
        functools.partial(kernel_body, nx, ny, scale, chunk),
        out_shape=(
            jax.ShapeDtypeStruct((wx, wy, ch), BF16),
            jax.ShapeDtypeStruct((depth, wx, wy, ch), BF16),
            jax.ShapeDtypeStruct((PARTS, chunk, ch), F32),
        ),
        in_specs=[hbm, hbm, hbm, hbm],
        out_specs=(vmem,) * 3,
        scratch_shapes=[
            pltpu.VMEM((depth, wx, wy, ch), BF16),
            pltpu.VMEM((depth, 3, 3, gw, ch), BF16),
            pltpu.VMEM((1, ch), F32),
            pltpu.VMEM((wx, wy, ch), BF16),
            pltpu.VMEM((2, 16, ch), BF16),
            pltpu.VMEM((2, 3, 16, ch), BF16),
            pltpu.VMEM((2, wy, ch), BF16),
            pltpu.VMEM((2, depth, wy, ch), BF16),
            pltpu.VMEM((depth, 3, 3 * ch, ch), BF16),
            pltpu.VMEM((3, depth * ch, 3 * ch), BF16),
            pltpu.VMEM((depth * ch, cells), BF16),
            pltpu.VMEM(((wx + 2) * wy, 3 * ch), BF16),
            pltpu.VMEM((depth, (wx + 2) * wy, 3 * ch), BF16),
            pltpu.VMEM((PARTS, chunk, ch), F32),
            pltpu.VMEM((PARTS - 1, chunk, ch), F32),
            pltpu.VMEM((nb, chunk, ch), F32),
            dma((4,)), dma((10,)), dma((10,)),
            dma((2, PARTS - 1)), dma((2, PARTS - 1)),
            dma((2, max(nb - 1, 1))), dma((2, max(nb - 1, 1))),
            dma((2, PARTS - 1)), dma((2, PARTS - 1)),
        ],
        compiler_params=pltpu.CompilerParams(
            collective_id=0, has_side_effects=True, vmem_limit_bytes=32 * 1024 * 1024
        ),
    )(*(pltpu.with_memory_space_constraint(x, pltpu.HBM) for x in (planes, kernel, bias.reshape(1, ch), cotangent)))
    return out, grad, sums.reshape(PARTS * chunk, ch)


def by_owner(nx, planes, kernel, bias, cotangent):
    depth, wx, wy, ch = planes.shape
    cells = wx * wy
    gw = ch // GROUPS
    lanes = 2 * wy
    nb = nx // LOW_X
    scale = np.float32(1.0) / np.sqrt(np.float32(cells * nx * 2))
    dma = pltpu.SemaphoreType.DMA
    vmem = pl.BlockSpec(memory_space=pltpu.VMEM)
    hbm = pl.BlockSpec(memory_space=pltpu.HBM)
    return pl.pallas_call(
        functools.partial(owner_body, nx, scale),
        out_shape=(
            jax.ShapeDtypeStruct((wx, wy, ch), BF16),
            jax.ShapeDtypeStruct((depth, wx, wy, ch), BF16),
            jax.ShapeDtypeStruct((depth * 9 * gw + 8, ch), F32),
        ),
        in_specs=[hbm, hbm, hbm, hbm],
        out_specs=(vmem,) * 3,
        scratch_shapes=[
            pltpu.VMEM((depth, wx, wy, ch), BF16),
            pltpu.VMEM((depth, 3, 3, gw, ch), BF16),
            pltpu.VMEM((1, ch), F32),
            pltpu.VMEM((wx, wy, ch), BF16),
            pltpu.VMEM((2, 16, ch), BF16),
            pltpu.VMEM((2, 3, 16, ch), BF16),
            pltpu.VMEM((2, wy, ch), BF16),
            pltpu.VMEM((2, depth, wy, ch), BF16),
            pltpu.VMEM((depth, 3, 3 * ch, ch), BF16),
            pltpu.VMEM((3, depth * ch, 3 * ch), BF16),
            pltpu.VMEM(((wx + 2) * wy, 3 * ch), BF16),
            pltpu.VMEM((depth, (wx + 2) * wy, 3 * ch), BF16),
            pltpu.VMEM((GROUPS, (depth + 1) * gw, cells), BF16),
            pltpu.VMEM((PIECES, PARTS, (depth + 1) * gw, cells), BF16),
            pltpu.VMEM((PIECES, 2, 2, (depth + 1) * gw, lanes), BF16),
            pltpu.VMEM(((depth + 1) * gw, (LOW_X * wx + 1) * lanes), BF16),
            pltpu.VMEM((2 * ch, (LOW_X * wx + 1) * lanes), BF16),
            pltpu.VMEM((PIECES, nb, depth * gw + 8, ch), F32),
            pltpu.VMEM((GROUPS, depth * gw + 8, ch), F32),
            dma((3 + depth,)), dma((10,)), dma((10,)),
            dma((PIECES, OWNERS)), dma((PIECES, PARTS)),
            dma((PIECES, OWNERS)), dma((PIECES, 2, 2)),
            dma((PIECES, nb - 1)), dma((PIECES, nb - 1)),
            dma((PIECES, PARTS - 1)), dma((GROUPS,)),
            pltpu.SemaphoreType.REGULAR,
        ],
        compiler_params=pltpu.CompilerParams(
            collective_id=0, has_side_effects=True, vmem_limit_bytes=32 * 1024 * 1024
        ),
    )(*(pltpu.with_memory_space_constraint(x, pltpu.HBM) for x in (planes, kernel, bias.reshape(1, ch), cotangent)))


def shards(nx, ny, planes, kernel, bias, cotangent):
    depth, wx, wy, ch = planes.shape
    gw = ch // GROUPS
    if ny == 2 and nx == 4 * LOW_X and (depth, wx, 2 * wy, ch, gw) == (3, 4, 128, 128, 16):
        out, grad, sums = by_owner(nx, planes, kernel, bias, cotangent)
    else:
        out, grad, sums = by_part(nx, ny, planes, kernel, bias, cotangent)
    dma = pltpu.SemaphoreType.DMA
    vmem = pl.BlockSpec(memory_space=pltpu.VMEM)
    hbm = pl.BlockSpec(memory_space=pltpu.HBM)
    base = depth * 9 * gw
    out, grad, kernel_grad, bias_grad = pl.pallas_call(
        place_body,
        out_shape=(
            jax.ShapeDtypeStruct(out.shape, BF16),
            jax.ShapeDtypeStruct(grad.shape, BF16),
            jax.ShapeDtypeStruct((base, ch), F32),
            jax.ShapeDtypeStruct((1, ch), F32),
        ),
        in_specs=[vmem] * 3,
        out_specs=(hbm, hbm, hbm, hbm),
        scratch_shapes=[dma((4,))],
    )(*(pltpu.with_memory_space_constraint(x, pltpu.VMEM) for x in (out, grad, sums)))
    return out, grad, kernel_grad.reshape(kernel.shape), bias_grad.reshape(ch)


def solution(mesh):
    in_specs = (P(None, "gx", "gy", None), P(), P(), P("gx", "gy", None))
    out_specs = (P("gx", "gy", None), P(None, "gx", "gy", None), P(), P())
    body = functools.partial(shards, mesh.shape["gx"], mesh.shape["gy"])
    return jax.shard_map(body, mesh=mesh, in_specs=in_specs, out_specs=out_specs, check_vma=False)
```
